256 devices in a mesh: row: 4 (over z_lo, core), col: 16 (over y, x), depth: 4 (over z_hi).
Axes of the slice: x: 4, y: 4, z: 8 (z_hi: 4, z_lo: 2; z = z_hi * 2 + z_lo), core: 2. Of those that a mesh axis runs over, the one named last changes fastest.
Arguments:
- diag_two: float32 [256, 256], replicated, may hold values from -3 to 3, as said below
- diag_one: float32 [256, 256], replicated, may hold values from -3 to 3, as said below
- cross_tile: float32 [256, 256], replicated, may hold values from -0.375 to 0.375
- left_two: float32 [256, 32768], P(None, ('col', 'depth')), may hold values from -0.375 to 0.375
- left_one: float32 [256, 32768], P(None, ('col', 'depth')), may hold values from -0.375 to 0.375
- below_left: float32 [4096, 32768], P('row', ('col', 'depth')), may hold values from -0.09375 to 0.09375
- panel_two: float32 [4096, 256], P('row', 'col'), may hold values from -0.09375 to 0.09375
- panel_one: float32 [4096, 256], P('row', 'col'), may hold values from -0.09375 to 0.09375
- grad_diag_two: float32 [256, 256], replicated, may hold values from -6 to 6
- grad_diag_one: float32 [256, 256], replicated, may hold values from -6 to 6
- grad_cross: float32 [256, 256], replicated, may hold values from -6 to 6
- grad_left_two: float32 [256, 32768], P('row', ('col', 'depth')), may hold values from -6 to 6
- grad_left_one: float32 [256, 32768], P('row', ('col', 'depth')), may hold values from -6 to 6
- grad_below: float32 [4096, 32768], P('row', ('col', 'depth')), may hold values from -6 to 6
- grad_panel_two: float32 [4096, 256], P('row', 'col'), may hold values from -6 to 6
- grad_panel_one: float32 [4096, 256], P('row', 'col'), may hold values from -6 to 6
Outputs:
- out_below: float32 [4096, 32768], P('row', ('col', 'depth'))
- out_left_two: float32 [256, 32768], P('row', ('col', 'depth'))
- out_left_one: float32 [256, 32768], P('row', ('col', 'depth'))
- out_diag_two: float32 [256, 256], replicated
- out_diag_one: float32 [256, 256], replicated
- out_cross: float32 [256, 256], replicated
- out_panel_two: float32 [4096, 256], P('row', 'col')
- out_panel_one: float32 [4096, 256], P('row', 'col')
The draws below stay inside these ranges and needn't reach their ends.
Inputs may be any that keep to these rules, and one draw needn't show every extreme that they name: `diag_two`: lower triangular; its diagonal lies in 1 to 3. `diag_one`: lower triangular; its diagonal lies in 1 to 3.
All inputs are finite; a program needn't handle non-finite values.
Results may differ from the reference program's by a relative error of at most 0.000071.
Values sent between devices are 32-bit elements; how exact they have to be, the bound alone decides.
No kernel may reach another device: no remote copies, remote signals or barrier semaphores. Data moves between devices by JAX's collectives and lax.ppermute only.
A program may use at most 64 MiB of HBM per device.

```python
import math
import jax
import jax.numpy as jnp
from jax import lax

P_SIZE = 256
M = 4096
J = 32768


def lower_factor(key):
    first, second = jax.random.split(key)
    diagonal = jnp.exp(jax.random.uniform(first, (P_SIZE,), jnp.float32, 0.0, math.log(3.0)))
    below = jnp.clip(jax.random.normal(second, (P_SIZE, P_SIZE), jnp.float32), -5.0, 5.0) * (0.5 / math.sqrt(P_SIZE))
    return jnp.tril(below, -1) + jnp.diag(diagonal)


def draw_diag_two(key, part):
    return lower_factor(jax.random.fold_in(key, 2))


def draw_diag_one(key, part):
    return lower_factor(jax.random.fold_in(key, 1))


def steps_of(key, extent, shards, low, largest):
    loudness = 1.0
    for axis_at, parts in shards:
        heights = jax.random.uniform(jax.random.fold_in(jax.random.fold_in(key, 6), axis_at), (parts,), jnp.float32, low / len(shards), largest / len(shards))
        loudness = loudness * jnp.repeat(jnp.exp(heights), extent[axis_at] // parts).reshape((-1,) + (1,) * (len(extent) - 1 - axis_at))
    return loudness


def scatter_about(stream_key, dims, scale, limit, cuts=(), held_as=jnp.bfloat16):
    level = steps_of(stream_key, dims, cuts, -0.22, 0.18) if cuts else 1.0
    drawn = jax.random.normal(stream_key, dims, jnp.float32) * scale * level
    return jnp.minimum(jnp.maximum(drawn, -limit), limit).astype(held_as)


def setup_inputs(seed: int = 0) -> dict:
    streams_of = jax.random.split(jax.random.key(seed), 17)
    return {
        "diag_two": draw_diag_two(jax.random.fold_in(streams_of[16], 71), 0),
        "diag_one": draw_diag_one(jax.random.fold_in(streams_of[16], 71), 0),
        "cross_tile": scatter_about(streams_of[2], (P_SIZE, P_SIZE), P_SIZE ** -0.5, 0.375, (), jnp.float32),
        "left_two": scatter_about(streams_of[3], (P_SIZE, J), P_SIZE ** -0.5, 0.375, ((1, 64),), jnp.float32),
        "left_one": scatter_about(streams_of[4], (P_SIZE, J), P_SIZE ** -0.5, 0.375, ((1, 64),), jnp.float32),
        "below_left": scatter_about(streams_of[5], (M, J), M ** -0.5, 0.09375, ((0, 4), (1, 64)), jnp.float32),
        "panel_two": scatter_about(streams_of[6], (M, P_SIZE), M ** -0.5, 0.09375, ((0, 4), (1, 16)), jnp.float32),
        "panel_one": scatter_about(streams_of[7], (M, P_SIZE), M ** -0.5, 0.09375, ((0, 4), (1, 16)), jnp.float32),
        "grad_diag_two": scatter_about(streams_of[8], (P_SIZE, P_SIZE), 1.0, 6.0, (), jnp.float32),
        "grad_diag_one": scatter_about(streams_of[9], (P_SIZE, P_SIZE), 1.0, 6.0, (), jnp.float32),
        "grad_cross": scatter_about(streams_of[10], (P_SIZE, P_SIZE), 1.0, 6.0, (), jnp.float32),
        "grad_left_two": scatter_about(streams_of[11], (P_SIZE, J), 1.0, 6.0, ((0, 4), (1, 64)), jnp.float32),
        "grad_left_one": scatter_about(streams_of[12], (P_SIZE, J), 1.0, 6.0, ((0, 4), (1, 64)), jnp.float32),
        "grad_below": scatter_about(streams_of[13], (M, J), 1.0, 6.0, ((0, 4), (1, 64)), jnp.float32),
        "grad_panel_two": scatter_about(streams_of[14], (M, P_SIZE), 1.0, 6.0, ((0, 4), (1, 16)), jnp.float32),
        "grad_panel_one": scatter_about(streams_of[15], (M, P_SIZE), 1.0, 6.0, ((0, 4), (1, 16)), jnp.float32),
    }


def matmul(left, right):
    return jnp.dot(left.astype(jnp.float32), right.astype(jnp.float32), precision=lax.Precision.HIGHEST, preferred_element_type=jnp.float32)

def right_solve(factor, values):
    return lax.linalg.triangular_solve(factor, values, left_side=False, lower=True)

def halved(square):
    return jnp.tril(square) - 0.5 * jnp.diag(jnp.diag(square))

def reverse_block(factor, cotangent):
    inner = halved(matmul(factor.T, cotangent))
    leftward = lax.linalg.triangular_solve(factor, inner, left_side=True, lower=True, transpose_a=True)
    spread = right_solve(factor, leftward)
    return spread + spread.T

def reference(diag_two, diag_one, cross_tile, left_two, left_one, below_left, panel_two, panel_one, grad_diag_two, grad_diag_one, grad_cross, grad_left_two, grad_left_one, grad_below, grad_panel_two, grad_panel_one):
    solved_two = right_solve(diag_two, grad_panel_two)
    below_first = grad_below - matmul(solved_two, left_two)
    panel_next = grad_panel_one - matmul(solved_two, cross_tile)
    gram_two = matmul(solved_two.T, panel_two)
    gram_cross = matmul(solved_two.T, panel_one)
    sym_two = reverse_block(diag_two, grad_diag_two - jnp.tril(gram_two))
    cross_next = grad_cross - gram_cross - matmul(sym_two, cross_tile)
    out_cross = right_solve(diag_one, cross_next)
    out_panel_one = right_solve(diag_one, panel_next)
    out_below = below_first - matmul(out_panel_one, left_one)
    gram_one = matmul(out_cross.T, cross_tile) + matmul(out_panel_one.T, panel_one)
    sym_one = reverse_block(diag_one, grad_diag_one - jnp.tril(gram_one))
    out_left_two = grad_left_two - matmul(solved_two.T, below_left) - matmul(sym_two, left_two) - matmul(out_cross, left_one)
    out_left_one = grad_left_one - matmul(out_cross.T, left_two) - matmul(out_panel_one.T, below_left) - matmul(sym_one, left_one)
    return (out_below, out_left_two, out_left_one, halved(sym_two), halved(sym_one), out_cross, solved_two, out_panel_one)
```

```python
import jax
import jax.numpy as jnp
from jax import lax
from jax.experimental import pallas as pl
from jax.experimental.pallas import tpu as pltpu
from jax.sharding import Mesh, PartitionSpec as P

F32 = jnp.float32
BF16 = jnp.bfloat16
VMEM = pl.BlockSpec(memory_space=pltpu.VMEM)
SMEM = pl.BlockSpec(memory_space=pltpu.SMEM)
NN = (((1,), (0,)), ((), ()))
NT = (((1,), (1,)), ((), ()))
TN = (((0,), (0,)), ((), ()))


def full(a, b, dims=NN):
    return lax.dot_general(a, b, dims, precision=lax.Precision.HIGHEST, preferred_element_type=F32)


def one(a, b, dims=NN):
    return lax.dot_general(a, b, dims, preferred_element_type=F32)


def split(a):
    hi = a.astype(BF16)
    return hi, (a - hi.astype(F32)).astype(BF16)


def dot3(a, b, dims=NN):
    return one(a[0], b[0], dims) + (one(a[0], b[1], dims) + one(a[1], b[0], dims))


def shaped(*shape, dtype=F32):
    return jax.ShapeDtypeStruct(shape, dtype)


def params():
    return pltpu.CompilerParams(vmem_limit_bytes=56 * 2**20)


def positions(n):
    return (
        lax.broadcasted_iota(jnp.int32, (n, n), 0),
        lax.broadcasted_iota(jnp.int32, (n, n), 1),
    )


def halved(square):
    row, col = positions(square.shape[0])
    return jnp.where(row > col, square, jnp.where(row == col, 0.5 * square, 0.0))


def inverse_kernel(d2, d1, c, l2, l1, a2, a2t, a1, a1t, d2t, d1t, vt, w_hi, w_lo):
    n = d2.shape[0]
    row, col = positions(n)
    factors = (d2[...], d1[...])
    xs = [jnp.where(row == col, 1.0 / f, 0.0) for f in factors]
    step = 0
    while (1 << step) < n:
        inside = (
            ((row >> (step + 1)) == (col >> (step + 1)))
            & ((row >> step) != (col >> step))
            & (row > col)
        )
        parts = [full(jnp.where(inside, f, 0.0), x) for f, x in zip(factors, xs)]
        xs = [x - full(x, p) for x, p in zip(xs, parts)]
        step += 1
    x2, x1 = xs
    a2[...] = x2
    a1[...] = x1
    x2t, x1t = (x2.T, x1.T)
    a2t[...] = x2t
    a1t[...] = x1t
    d2t[...] = factors[0].T
    d1t[...] = factors[1].T
    vt[0, :, :n] = x2t
    vt[0, :, n:] = jnp.zeros((n, n), F32)
    vt[1, :, :n] = -full(x2, full(c[...], x1)).T
    vt[1, :, n:] = x1t
    w1 = full(x1, l1[...])
    w2 = full(x2, l2[...] - full(c[...], w1))
    hi, lo = split(w1)
    w_hi[n:] = hi
    w_lo[n:] = lo
    hi, lo = split(w2)
    w_hi[:n] = hi
    w_lo[:n] = lo


def inverses(d2, d1, c, l2, l1):
    n, width = l2.shape
    square = shaped(n, n)
    return pl.pallas_call(
        inverse_kernel,
        out_shape=(square,) * 6
        + (shaped(2, n, 2 * n), shaped(2 * n, width, dtype=BF16), shaped(2 * n, width, dtype=BF16)),
        in_specs=[VMEM] * 5,
        out_specs=[VMEM] * 9,
        compiler_params=params(),
        name="inverses",
    )(d2, d1, c, l2, l1)


def split_kernel(a, hi, lo):
    hi[...], lo[...] = split(a[...])


def split_rows(a):
    rows, cols = a.shape
    spec = pl.BlockSpec((rows // 4, cols), lambda i: (i, 0))
    return pl.pallas_call(
        split_kernel,
        grid=(4,),
        out_shape=(shaped(rows, cols, dtype=BF16),) * 2,
        in_specs=[spec],
        out_specs=[spec] * 2,
        compiler_params=params(),
        name="split_rows",
    )(a)


def gram_kernel(place, p2, p1, own, x1, x2, x3, y1, y2, y3, dy1, dy2, dy3, dx1, dx2, dx3, hi, lo, gram):
    x, y = (place[0], place[1])
    n = hi.shape[0] // 2
    w = p2.shape[0]

    def put(values, half, xx, yy):
        at = pl.multiple_of(half * n + ((yy & 3) * 4 + (xx & 3)) * w, w)
        h, l = split(values)
        hi[pl.ds(at, w)] = h
        lo[pl.ds(at, w)] = l

    for half in range(2):
        rows = pl.ds(half * w, w)
        put(own[rows], half, x, y)
        for k, ref in enumerate((x1, x2, x3)):
            put(ref[rows], half, x + 3 - k, y)
        for k, ref in enumerate((y1, y2, y3)):
            put(ref[rows], half, x, y + 3 - k)
    for k, ref in enumerate((dy1, dy2, dy3)):
        for j in range(3):
            put(ref[pl.ds(j * w, w)], 0, x + 3 - j, y + 3 - k)
    for k, ref in enumerate((dx1, dx2, dx3)):
        for j in range(3):
            put(ref[pl.ds(j * w, w)], 1, x + 3 - k, y + 3 - j)
    p2s, p1s = (split(p2[...]), split(p1[...]))
    both = tuple(jnp.concatenate(pair, axis=0) for pair in zip(p2s, p1s))
    gram[: 2 * w] = dot3(both, (hi[:n], lo[:n]), NT)
    gram[2 * w :] = dot3(p1s, (hi[n:], lo[n:]), NT)


def grams(place, p2, p1, pieces, n):
    rows = p2.shape[1]
    w = p2.shape[0]
    return pl.pallas_call(
        gram_kernel,
        out_shape=(
            shaped(2 * n, rows, dtype=BF16),
            shaped(2 * n, rows, dtype=BF16),
            shaped(3 * w, n),
        ),
        in_specs=[SMEM] + [VMEM] * (2 + len(pieces)),
        out_specs=[VMEM] * 3,
        compiler_params=params(),
        name="grams",
    )(place, p2, p1, *pieces)


def below_sum_kernel(place, hi, lo, bl_hi, bl_lo, a2t, a1t, c, keep, send):
    n = a2t.shape[0]
    share = n // 4
    below = (bl_hi[...], bl_lo[...])
    q2 = dot3((hi[:n], lo[:n]), below)
    u2 = dot3(split(a2t[...]), split(q2))
    q1 = dot3((hi[n:], lo[n:]), below)
    q1 = q1 - dot3(split(c[...].T), split(u2))
    u1 = dot3(split(a1t[...]), split(q1))
    for core in range(2):

        @pl.when(place[2] == core)
        def _():
            for r in range(4):
                ref = keep if r % 2 == core else send
                ref[r // 2, :share] = u2[r * share : (r + 1) * share]
                ref[r // 2, share:] = u1[r * share : (r + 1) * share]


def below_sums(place, hi, lo, bl_hi, bl_lo, a2t, a1t, c):
    n = a2t.shape[0]
    width = bl_hi.shape[1]
    return pl.pallas_call(
        below_sum_kernel,
        out_shape=(shaped(2, n // 2, width),) * 2,
        in_specs=[SMEM] + [VMEM] * 7,
        out_specs=[VMEM] * 2,
        compiler_params=params(),
        name="below_sums",
    )(place, hi, lo, bl_hi, bl_lo, a2t, a1t, c)


def pair_kernel(place, keep, got, mine, send):
    z = place[3]
    mine[...] = (keep[pl.ds(z, 1)] + got[pl.ds(z, 1)])[0]
    send[...] = (keep[pl.ds(1 - z, 1)] + got[pl.ds(1 - z, 1)])[0]


def pair_sums(place, keep, got):
    return pl.pallas_call(
        pair_kernel,
        out_shape=(shaped(*keep.shape[1:]),) * 2,
        in_specs=[SMEM] + [VMEM] * 2,
        out_specs=[VMEM] * 2,
        compiler_params=params(),
        name="pair_sums",
    )(place, keep, got)


def below_kernel(place, hi, lo, w_hi, w_lo, vt, grad, out, s2t, s1t):
    w = s2t.shape[0]
    g = (hi[...], lo[...])
    out[...] = grad[...] - dot3(g, (w_hi[...], w_lo[...]), TN)
    at = pl.multiple_of((place[1] * 4 + place[0]) * w, w)
    v = jnp.concatenate([vt[0, pl.ds(at, w)], vt[1, pl.ds(at, w)]], axis=0)
    solved = dot3(split(v), g)
    s2t[...] = solved[:w]
    s1t[...] = solved[w:]


def below_outputs(place, hi, lo, w_hi, w_lo, vt, grad, w):
    rows, width = grad.shape
    steps = 4
    tall = rows // steps
    whole = lambda a: pl.BlockSpec(a.shape, lambda i: (0,) * a.ndim)
    across = pl.BlockSpec((hi.shape[0], tall), lambda i: (0, i))
    thin = pl.BlockSpec((w, tall), lambda i: (0, i))
    block = pl.BlockSpec((tall, width), lambda i: (i, 0))
    return pl.pallas_call(
        below_kernel,
        grid=(steps,),
        out_shape=(shaped(rows, width), shaped(w, rows), shaped(w, rows)),
        in_specs=[SMEM, across, across, whole(w_hi), whole(w_lo), whole(vt), block],
        out_specs=[block, thin, thin],
        compiler_params=params(),
        name="below_outputs",
    )(place, hi, lo, w_hi, w_lo, vt, grad)


def chain_kernel(
    place, mine, other, a2, a2t, a1, a1t, d2t, d1t, c, gd2, gd1, gc, l2, l1, gl2, gl1, part, got,
    o_left2, o_left1, o_diag2, o_diag1, o_cross, rows2, rows1, rowsx, rowsxt,
):
    n = a2.shape[0]
    w = mine.shape[1] // 3
    first = place[2] == 0
    a, b = (mine[...], other[...])
    low = jnp.where(first, a, b)
    high = jnp.where(first, b, a)

    def gathered(k):
        return jnp.concatenate(
            [half[:, k * w : (k + 1) * w].reshape(n, n // 2) for half in (low, high)], axis=1
        )

    row, col = positions(n)
    lower = row >= col
    gram2 = full(gathered(0), a2[...]).T
    cross_t = full(gathered(1), a2[...])
    below_t = full(gathered(2) - full(cross_t, c[...]), a1[...])
    inner = halved(full(d2t[...], gd2[...] - jnp.where(lower, gram2, 0.0)))
    spread = full(full(a2t[...], inner), a2[...])
    sym2 = spread + spread.T
    rows2[...] = sym2
    o_diag2[...] = halved(sym2)
    cross = full(gc[...] - cross_t.T - full(sym2, c[...]), a1[...])
    o_cross[...] = cross
    rowsx[...] = cross
    cross_turned = cross.T
    rowsxt[...] = cross_turned
    gram1 = full(cross_turned, c[...]) + below_t.T
    inner = halved(full(d1t[...], gd1[...] - jnp.where(lower, gram1, 0.0)))
    spread = full(full(a1t[...], inner), a1[...])
    sym1 = spread + spread.T
    rows1[...] = sym1
    o_diag1[...] = halved(sym1)
    share = gl2.shape[0]
    at = pl.ds(pl.multiple_of((place[3] * 2 + place[2]) * share, share), share)
    l2s, l1s = (split(l2[...]), split(l1[...]))
    o_left2[...] = (
        gl2[...]
        - (part[:share] + got[:share])
        - dot3(split(rows2[at]), l2s)
        - dot3(split(rowsx[at]), l1s)
    )
    o_left1[...] = (
        gl1[...]
        - dot3(split(rowsxt[at]), l2s)
        - (part[share:] + got[share:])
        - dot3(split(rows1[at]), l1s)
    )


def chain(place, *operands):
    n = operands[2].shape[0]
    left = operands[14].shape
    return pl.pallas_call(
        chain_kernel,
        out_shape=(shaped(*left), shaped(*left), shaped(n, n), shaped(n, n), shaped(n, n)),
        in_specs=[SMEM] + [VMEM] * len(operands),
        out_specs=[VMEM] * 5,
        scratch_shapes=[pltpu.VMEM((n, n), F32)] * 4,
        compiler_params=params(),
        name="chain",
    )(place, *operands)


def shifted(value, axis, by):
    count = lax.axis_size(axis)
    return lax.ppermute(value, axis, [(i, (i + by) % count) for i in range(count)])


def shared(value, axes):
    count = lax.axis_size(axes)
    return lax.all_to_all(
        jnp.broadcast_to(value[None], (count, *value.shape)), axes, 0, 0, tiled=True
    )


def body(d2, d1, c, l2, l1, bl, p2, p1, gd2, gd1, gc, gl2, gl1, gb, g2, g1):
    n = d2.shape[0]
    w = p2.shape[1]
    core = lax.axis_index("core")
    place = jnp.stack(
        [lax.axis_index("x"), lax.axis_index("y"), core, lax.axis_index("zlo")]
    ).astype(jnp.int32)
    own = jnp.concatenate([g2.T, g1.T], axis=0)
    xs = [shifted(own, "x", k) for k in (1, 2, 3)]
    ys = [shifted(own, "y", k) for k in (1, 2, 3)]
    a2, a2t, a1, a1t, d2t, d1t, vt, w_hi, w_lo = inverses(d2, d1, c, l2, l1)
    bl_hi, bl_lo = split_rows(bl)
    from_x = jnp.concatenate([v[:w] for v in xs], axis=0)
    from_y = jnp.concatenate([v[w:] for v in ys], axis=0)
    dys = [shifted(from_x, "y", k) for k in (1, 2, 3)]
    dxs = [shifted(from_y, "x", k) for k in (1, 2, 3)]
    hi, lo, gram = grams(place, p2.T, p1.T, [own, *xs, *ys, *dys, *dxs], n)
    gram = shared(gram, ("zlo", "core")).sum(axis=0)
    gram = shared(lax.dynamic_slice_in_dim(gram, core * (n // 2), n // 2, 1), ("y", "x"))
    other = shifted(gram, "core", 1)
    keep, send = below_sums(place, hi, lo, bl_hi, bl_lo, a2t, a1t, c)
    part, send = pair_sums(place, keep, shifted(send, "core", 1))
    got = shifted(send, "zlo", 1)
    out_below, s2t, s1t = below_outputs(place, hi, lo, w_hi, w_lo, vt, gb, w)
    left2, left1, diag2, diag1, cross = chain(
        place, gram, other, a2, a2t, a1, a1t, d2t, d1t, c, gd2, gd1, gc, l2, l1, gl2, gl1, part, got
    )
    return out_below, left2, left1, diag2, diag1, cross, s2t.T, s1t.T


def solution(mesh):
    fine = Mesh(
        mesh.devices.reshape(2, 2, 4, 4, 4), ("zlo", "core", "y", "x", "dep")
    )
    row, col, deep = (("zlo", "core"), ("y", "x"), ("y", "x", "dep"))
    return jax.shard_map(
        body,
        mesh=fine,
        in_specs=(
            P(),
            P(),
            P(),
            P(None, deep),
            P(None, deep),
            P(row, deep),
            P(row, col),
            P(row, col),
            P(),
            P(),
            P(),
            P(row, deep),
            P(row, deep),
            P(row, deep),
            P(row, col),
            P(row, col),
        ),
        out_specs=(
            P(row, deep),
            P(row, deep),
            P(row, deep),
            P(),
            P(),
            P(),
            P(row, col),
            P(row, col),
        ),
        check_vma=False,
    )
```

```python
import jax
import jax.numpy as jnp
from jax import lax
from jax.experimental import pallas as pl
from jax.experimental.pallas import tpu as pltpu
from jax.sharding import Mesh, PartitionSpec as P

F32 = jnp.float32
BF16 = jnp.bfloat16
VMEM = pl.BlockSpec(memory_space=pltpu.VMEM)
SMEM = pl.BlockSpec(memory_space=pltpu.SMEM)
NN = (((1,), (0,)), ((), ()))
NT = (((1,), (1,)), ((), ()))
TN = (((0,), (0,)), ((), ()))


def full(a, b, dims=NN):
    return lax.dot_general(a, b, dims, precision=lax.Precision.HIGHEST, preferred_element_type=F32)


def one(a, b, dims=NN):
    return lax.dot_general(a, b, dims, preferred_element_type=F32)


def split(a):
    hi = a.astype(BF16)
    return hi, (a - hi.astype(F32)).astype(BF16)


def dot3(a, b, dims=NN):
    return one(a[0], b[0], dims) + (one(a[0], b[1], dims) + one(a[1], b[0], dims))


def shaped(*shape, dtype=F32):
    return jax.ShapeDtypeStruct(shape, dtype)


def near(*shape, dtype=F32):
    return pltpu.VMEM(shape, dtype)


def call(kernel, name, outs, operands, scratch=(), micros=2.0, loads=0, space=pltpu.VMEM, out_specs=None):
    kept = len(operands) - loads
    held = [pltpu.with_memory_space_constraint(v, pltpu.VMEM) for v in operands[1:kept]]
    far = [pltpu.with_memory_space_constraint(v, pltpu.HBM) for v in operands[kept:]]
    return pl.pallas_call(
        kernel,
        out_shape=tuple(outs),
        in_specs=[SMEM] + [VMEM] * len(held) + [pl.BlockSpec(memory_space=space)] * loads,
        out_specs=out_specs or [VMEM] * len(outs),
        scratch_shapes=list(scratch),
        compiler_params=pltpu.CompilerParams(vmem_limit_bytes=20 * 2**20),
        cost_estimate=pl.CostEstimate(
            flops=int(micros * 1e9), transcendentals=0, bytes_accessed=int(micros * 3e6)
        ),
        name=name,
    )(operands[0], *held, *far)


def positions(n):
    return (
        lax.broadcasted_iota(jnp.int32, (n, n), 0),
        lax.broadcasted_iota(jnp.int32, (n, n), 1),
    )


def halved(square):
    row, col = positions(square.shape[0])
    return jnp.where(row > col, square, jnp.where(row == col, 0.5 * square, 0.0))


def three(a):
    hi = a.astype(BF16)
    rest = a - hi.astype(F32)
    mid = rest.astype(BF16)
    return hi, mid, (rest - mid.astype(F32)).astype(BF16)


def dot3f(a, b, dims=NN):
    return dot3(split(a), split(b), dims)


def block_inverses(factor, size):
    n = factor.shape[0]
    row, col = positions(n)
    same = (row // size) == (col // size)
    lower = jnp.where(same & (row >= col), factor, 0.0)
    packed = lower[:size]
    for k in range(1, n // size):
        packed = packed + lower[k * size : (k + 1) * size]
    line = lax.broadcasted_iota(jnp.int32, (size, n), 0)
    lane = lax.broadcasted_iota(jnp.int32, (size, n), 1) % size
    columns = jnp.concatenate([jnp.where(lane == j, packed, 0.0) for j in range(size)], axis=0)
    ones = jnp.where(same, 1.0, 0.0).astype(BF16)
    hi, mid, lo = three(columns)
    spread = one(hi, ones) + (one(mid, ones) + one(lo, ones))
    x = jnp.where(line == lane, 1.0, 0.0)
    for j in range(size):
        column = spread[j * size : (j + 1) * size]
        solved = x[j : j + 1] / column[j : j + 1]
        x = jnp.where(line == j, solved, x - jnp.where(line > j, column, 0.0) * solved)
    return jnp.where(same, jnp.concatenate([x] * (n // size), axis=0), 0.0)


def inverses_of(factors):
    n = factors[0].shape[0]
    half = n // 2
    size = 16
    xs = [block_inverses(f, size) for f in factors]
    blocks = [(f, x, at) for f, x in zip(factors, xs) for at in (0, half)]
    corners = [x[at : at + half, at : at + half] for f, x, at in blocks]
    belows = [f[at : at + half, at : at + half] for f, x, at in blocks]
    row, col = positions(half)
    while size < half:
        inside = (row // (2 * size) == col // (2 * size)) & (row // size > col // size)
        parts = [full(jnp.where(inside, f, 0.0), x) for f, x in zip(belows, corners)]
        corners = [x - full(x, p) for x, p in zip(corners, parts)]
        size *= 2
    outs = []
    parts = [full(f[half:, :half], corners[2 * k]) for k, f in enumerate(factors)]
    parts = [full(corners[2 * k + 1], p) for k, p in enumerate(parts)]
    for k, p in enumerate(parts):
        top = jnp.concatenate([corners[2 * k], jnp.zeros((half, half), F32)], axis=1)
        low = jnp.concatenate([-p, corners[2 * k + 1]], axis=1)
        outs.append(jnp.concatenate([top, low], axis=0))
    return outs


def inverse_kernel(place, *refs):
    count = (len(refs) - 5) // 2
    sources, (a2, a2t, a1, a1t), targets, sems = (
        refs[:count],
        refs[count : count + 4],
        refs[count + 4 : -1],
        refs[-1],
    )
    copies = [
        pltpu.make_async_copy(source, target, sems.at[k])
        for k, (source, target) in enumerate(zip(sources, targets))
    ]
    for copy in copies:
        copy.start()
    copies[0].wait()
    copies[1].wait()
    x2, x1 = inverses_of([targets[0][...], targets[1][...]])
    a2[...] = x2
    a1[...] = x1
    a2t[...] = x2.T
    a1t[...] = x1.T
    for copy in copies[2:]:
        copy.wait()


def weight_kernel(place, a2, a2t, a1, a1t, d2, d1, c, l2, l1, bl, d2t, d1t, vt, w_hi, w_lo, bl_hi, bl_lo):
    n = d2.shape[0]
    d2t[...] = d2[...].T
    d1t[...] = d1[...].T
    x1 = split(a1[...])
    x2 = split(a2[...])
    cs = split(c[...])
    vt[0, :, :n] = a2t[...]
    vt[0, :, n:] = jnp.zeros((n, n), F32)
    vt[1, :, :n] = -dot3(x2, split(dot3(cs, x1))).T
    vt[1, :, n:] = a1t[...]
    w1 = dot3(x1, split(l1[...]))
    hi, lo = split(w1)
    w_hi[n:] = hi
    w_lo[n:] = lo
    hi, lo = split(dot3(x2, split(l2[...] - dot3(cs, (hi, lo)))))
    w_hi[:n] = hi
    w_lo[:n] = lo
    bl_hi[...], bl_lo[...] = split(bl[...])


def first_kernel(place, g2, g1, p2, p1, along_x, along_y):
    w = g2.shape[0]
    along_x[:w] = g1[...]
    along_x[w : 2 * w] = p2[...]
    along_x[2 * w :] = p1[...]
    along_y[...] = g2[...]


def far_kernel(place, x0, y0, x1, x3, x2, y1, y3, y2, far_x, far_y):
    w = y0.shape[0]
    for k, (fx, fy) in enumerate(((x0, y0), (x1, y1), (x2, y2), (x3, y3))):
        far_x[k * w : (k + 1) * w] = fy[...]
        far_y[k * w : (k + 1) * w] = fx[:w]


def gram_kernel(
    place, x0, y0, x1, x3, x2, y1, y3, y2, dx1, dx3, dx2, dy1, dy3, dy2, hi, lo, keep, send, p,
):
    x, y, core = (place[0], place[1], place[2])
    n = hi.shape[0] // 2
    w = y0.shape[0]

    def put(values, half, xx, yy):
        at = pl.multiple_of(half * n + ((yy & 3) * 4 + (xx & 3)) * w, w)
        h, l = split(values)
        hi[pl.ds(at, w)] = h
        lo[pl.ds(at, w)] = l

    for k, (fx, fy) in enumerate(((x0, y0), (x1, y1), (x2, y2), (x3, y3))):
        put(fy[...], 0, x, y + 4 - k)
        put(fx[:w], 1, x + 4 - k, y)
        rows = pl.ds(pl.multiple_of(((x + 4 - k) & 3) * w, w), w)
        p[0, rows] = fx[w : 2 * w]
        p[1, rows] = fx[2 * w :]
    for k, (fx, fy) in enumerate(((dx1, dy1), (dx2, dy2), (dx3, dy3))):
        for j in range(4):
            rows = slice(j * w, (j + 1) * w)
            put(fx[rows], 0, x + 3 - k, y + 4 - j)
            put(fy[rows], 1, x + 4 - j, y + 3 - k)
    both = split(jnp.concatenate([p[0], p[1]], axis=0))
    wide = dot3((hi[:n], lo[:n]), both, NT)
    tall = dot3((hi[n:], lo[n:]), split(p[1]), NT)
    half = n // 2
    packed = jnp.concatenate([wide, jnp.concatenate([tall[:half], tall[half:]], axis=1)], axis=0)
    part = packed.shape[0] // 2

    @pl.when(core == 0)
    def _():
        keep[...] = packed[:part]
        send[...] = packed[part:]

    @pl.when(core == 1)
    def _():
        keep[...] = packed[part:]
        send[...] = packed[:part]


def add_kernel(place, a, b, out):
    out[...] = a[...] + b[...]


def stack_kernel(place, a, b, c, d, out):
    out[0] = a[...]
    out[1] = b[...]
    out[2] = c[...]
    out[3] = d[...]


def below_sum_kernel(place, hi, lo, bl_hi, bl_lo, a2t, a1t, c, keep, send):
    core = place[2]
    n = a2t.shape[0]
    share = n // 4
    below = (bl_hi[...], bl_lo[...])
    q2 = dot3((hi[:n], lo[:n]), below)
    u2 = dot3f(a2t[...], q2)
    q1 = dot3((hi[n:], lo[n:]), below)
    u1 = dot3f(a1t[...], q1 - dot3f(c[...].T, u2))
    for k in range(2):

        @pl.when(core == k)
        def _():
            for r in range(4):
                ref = keep if r % 2 == k else send
                ref[r // 2, :share] = u2[r * share : (r + 1) * share]
                ref[r // 2, share:] = u1[r * share : (r + 1) * share]


def pair_kernel(place, keep, got, mine, send):
    z = place[3]
    mine[...] = (keep[pl.ds(z, 1)] + got[pl.ds(z, 1)])[0]
    send[...] = (keep[pl.ds(1 - z, 1)] + got[pl.ds(1 - z, 1)])[0]


def below_kernel(place, hi, lo, w_hi, w_lo, vt, grad, out, s2t, s1t, held, sems):
    w = s2t.shape[0]
    weights = (w_hi[...], w_lo[...])
    steps = sems.shape[0]
    tall = held.shape[0] // steps
    copies = []
    for k in range(steps):
        rows = pl.ds(k * tall, tall)
        held[rows] = grad[rows] - dot3((hi[:, rows], lo[:, rows]), weights, TN)
        copies.append(pltpu.make_async_copy(held.at[rows], out.at[rows], sems.at[k]))
        copies[-1].start()
    at = pl.multiple_of((place[1] * 4 + place[0]) * w, w)
    v = jnp.concatenate([vt[0, pl.ds(at, w)], vt[1, pl.ds(at, w)]], axis=0)
    solved = dot3(split(v), (hi[...], lo[...]))
    s2t[...] = solved[:w]
    s1t[...] = solved[w:]
    for copy in copies:
        copy.wait()


def chain_kernel(
    place, mine, other, a2, a2t, a1, a1t, d2t, d1t, c, gd2, gd1, gc, l2, l1, gl2, gl1,
    left2, left1, o_diag2, o_diag1, o_cross, whole, tall, rows2, rows1, rowsx, rowsxt,
):
    n = a2.shape[0]
    first = place[2] == 0
    quarter = n // 4
    half = n // 2
    for k, by in enumerate((0, 1, 3, 2)):
        y = (place[1] + 4 - by) & 3
        a, b = (mine[k], other[k])
        block = jnp.concatenate([jnp.where(first, a, b), jnp.where(first, b, a)], axis=0)
        whole[y] = block[:n]
        tall[y, :half] = block[n:, :quarter]
        tall[y, half:] = block[n:, quarter:]
    row, col = positions(n)
    lower = row >= col
    both = [dot3f(a2t[...], whole[y]) for y in range(4)]
    gram2 = jnp.concatenate([b[:, :quarter] for b in both], axis=1)
    gram_cross = jnp.concatenate([b[:, quarter:] for b in both], axis=1)
    tall = jnp.concatenate([tall[y] for y in range(4)], axis=1)
    below = dot3f(a1t[...], tall - dot3f(c[...].T, gram_cross))
    inner = halved(dot3f(d2t[...], gd2[...] - jnp.where(lower, gram2, 0.0)))
    spread = dot3f(dot3f(a2t[...], inner), a2[...])
    sym2 = spread + spread.T
    rows2[...] = sym2
    o_diag2[...] = halved(sym2)
    cross = dot3f(gc[...] - gram_cross - dot3f(sym2, c[...]), a1[...])
    o_cross[...] = cross
    rowsx[...] = cross
    cross_turned = cross.T
    rowsxt[...] = cross_turned
    gram1 = dot3f(cross_turned, c[...]) + below
    inner = halved(dot3f(d1t[...], gd1[...] - jnp.where(lower, gram1, 0.0)))
    spread = dot3f(dot3f(a1t[...], inner), a1[...])
    sym1 = spread + spread.T
    rows1[...] = sym1
    o_diag1[...] = halved(sym1)
    share = gl2.shape[0]
    at = pl.ds(pl.multiple_of((place[3] * 2 + place[2]) * share, share), share)
    l2s, l1s = (split(l2[...]), split(l1[...]))
    left2[...] = gl2[...] - dot3(split(rows2[at]), l2s) - dot3(split(rowsx[at]), l1s)
    left1[...] = gl1[...] - dot3(split(rowsxt[at]), l2s) - dot3(split(rows1[at]), l1s)


def left_kernel(place, left2, left1, part, got, o_left2, o_left1):
    share = left2.shape[0]
    o_left2[...] = left2[...] - (part[:share] + got[:share])
    o_left1[...] = left1[...] - (part[share:] + got[share:])


def shifted(value, axis, by):
    count = lax.axis_size(axis)
    return lax.ppermute(value, axis, [(i, (i + by) % count) for i in range(count)])


def shifts(value, axis):
    return [shifted(value, axis, k) for k in (1, 3, 2)]


def after(values, first):
    return lax.optimization_barrier((tuple(values), first))[0]


def body(d2, d1, c, l2, l1, bl, p2, p1, gd2, gd1, gc, gl2, gl1, gb, g2, g1):
    n = d2.shape[0]
    width = l2.shape[1]
    rows, w = p2.shape
    core = lax.axis_index("core")
    place = jnp.stack(
        [lax.axis_index("x"), lax.axis_index("y"), core, lax.axis_index("zlo")]
    ).astype(jnp.int32)
    along_x, along_y = call(
        first_kernel,
        "first",
        (near(3 * w, rows), near(w, rows)),
        (place, g2.T, g1.T, p2.T, p1.T),
        (),
        1.0,
        4,
    )
    xs = shifts(along_x, "x")
    ys = shifts(along_y, "y")
    square = near(n, n)
    given = after((d2, d1, c, l2, l1, bl, gd2, gd1, gc, gl2, gl1, gb), along_x)
    a2, a2t, a1, a1t, d2, d1, c, l2, l1, bl, gd2, gd1, gc, gl2, gl1, gb = call(
        inverse_kernel,
        "inverses",
        (square,) * 4 + tuple(near(*v.shape) for v in given),
        (place, *given),
        (pltpu.SemaphoreType.DMA((len(given),)),),
        4.0,
        len(given),
        pltpu.HBM,
    )
    pieces = (along_x, along_y, *xs, *ys)
    (x0,) = after((along_x,), a2)
    far_x, far_y = call(
        far_kernel, "far", (near(4 * w, rows),) * 2, (place, x0, *pieces[1:]), (), 0.6
    )
    dxs = shifts(far_x, "x")
    dys = shifts(far_y, "y")
    halves = (near(rows, width, dtype=BF16),) * 2
    thick = (near(2 * n, width, dtype=BF16),) * 2
    (bl,) = after((bl,), far_x)
    d2t, d1t, vt, w_hi, w_lo, bl_hi, bl_lo = call(
        weight_kernel,
        "weights",
        (square, square, near(2, n, 2 * n), *thick, *halves),
        (place, a2, a2t, a1, a1t, d2, d1, c, l2, l1, bl),
        (),
        2.7,
    )
    half = near(6 * n // 8, n // 2)
    (x0,) = after((along_x,), w_hi)
    hi, lo, keep, send = call(
        gram_kernel,
        "grams",
        (near(2 * n, rows, dtype=BF16),) * 2 + (half, half),
        (place, x0, *pieces[1:], *dxs, *dys),
        (pltpu.VMEM((2, 4 * w, rows), F32),),
        2.0,
    )
    (gram,) = call(
        add_kernel, "pair_gram", (half,), (place, keep, shifted(send, "core", 1)), (), 0.5
    )
    (below_hi,) = after((bl_hi,), gram)
    keep, send = call(
        below_sum_kernel,
        "below_sums",
        (near(2, n // 2, width),) * 2,
        (place, hi, lo, below_hi, bl_lo, a2t, a1t, c),
        (),
        3.0,
    )
    (gram,) = call(
        add_kernel,
        "row_gram",
        (half,),
        (place, *after((gram,), keep), shifted(gram, "zlo", 1)),
        (),
        0.6,
    )
    part, send = call(
        pair_kernel,
        "pair_sums",
        (near(n // 2, width),) * 2,
        (place, keep, shifted(send, "core", 1)),
        (),
        0.6,
    )
    got = shifted(send, "zlo", 1)
    (gb,) = after((gb,), (send, gram))
    out_below, s2t, s1t = call(
        below_kernel,
        "below_outputs",
        (shaped(rows, width), shaped(w, rows), shaped(w, rows)),
        (place, hi, lo, w_hi, w_lo, vt, gb),
        (pltpu.VMEM(gb.shape, F32), pltpu.SemaphoreType.DMA((4,))),
        3.8,
        out_specs=[pl.BlockSpec(memory_space=pltpu.HBM), VMEM, VMEM],
    )
    (mine,) = call(
        stack_kernel,
        "stack",
        (near(4, *half.shape),),
        (place, *after((gram,), s2t), *shifts(gram, "y")),
        (),
        0.8,
    )
    left2, left1, diag2, diag1, cross = call(
        chain_kernel,
        "chain",
        (near(*gl2.shape), near(*gl2.shape), shaped(n, n), shaped(n, n), shaped(n, n)),
        (place, mine, shifted(mine, "core", 1), a2, a2t, a1, a1t, d2t, d1t, c, gd2, gd1, gc, l2, l1, gl2, gl1),
        (pltpu.VMEM((4, n, n // 2), F32), pltpu.VMEM((4, n, n // 4), F32))
        + (pltpu.VMEM((n, n), F32),) * 4,
        5.2,
    )
    left2, left1 = call(
        left_kernel, "left", (shaped(*gl2.shape),) * 2, (place, left2, left1, part, got), (), 1.0
    )
    return out_below, left2, left1, diag2, diag1, cross, s2t.T, s1t.T


def solution(mesh):
    fine = Mesh(
        mesh.devices.reshape(2, 2, 4, 4, 4), ("zlo", "core", "y", "x", "dep")
    )
    row, col, deep = (("zlo", "core"), ("y", "x"), ("y", "x", "dep"))
    return jax.shard_map(
        body,
        mesh=fine,
        in_specs=(
            P(),
            P(),
            P(),
            P(None, deep),
            P(None, deep),
            P(row, deep),
            P(row, col),
            P(row, col),
            P(),
            P(),
            P(),
            P(row, deep),
            P(row, deep),
            P(row, deep),
            P(row, col),
            P(row, col),
        ),
        out_specs=(
            P(row, deep),
            P(row, deep),
            P(row, deep),
            P(),
            P(),
            P(),
            P(row, col),
            P(row, col),
        ),
        check_vma=False,
    )
```

```python
import jax
import jax.numpy as jnp
from jax import lax
from jax.experimental import pallas as pl
from jax.experimental.pallas import tpu as pltpu
from jax.sharding import Mesh, PartitionSpec as P

F32 = jnp.float32
BF16 = jnp.bfloat16
VMEM = pl.BlockSpec(memory_space=pltpu.VMEM)
SMEM = pl.BlockSpec(memory_space=pltpu.SMEM)
NN = (((1,), (0,)), ((), ()))
NT = (((1,), (1,)), ((), ()))
TN = (((0,), (0,)), ((), ()))


def full(a, b, dims=NN):
    return lax.dot_general(a, b, dims, precision=lax.Precision.HIGHEST, preferred_element_type=F32)


def one(a, b, dims=NN):
    return lax.dot_general(a, b, dims, preferred_element_type=F32)


def split(a):
    hi = a.astype(BF16)
    return hi, (a - hi.astype(F32)).astype(BF16)


def dot3(a, b, dims=NN):
    return one(a[0], b[0], dims) + (one(a[0], b[1], dims) + one(a[1], b[0], dims))


def shaped(*shape, dtype=F32):
    return jax.ShapeDtypeStruct(shape, dtype)


def near(*shape, dtype=F32):
    return pltpu.VMEM(shape, dtype)


def call(kernel, name, outs, operands, scratch=(), micros=2.0, loads=0, space=pltpu.VMEM, out_specs=None):
    kept = len(operands) - loads
    held = [pltpu.with_memory_space_constraint(v, pltpu.VMEM) for v in operands[1:kept]]
    far = [pltpu.with_memory_space_constraint(v, pltpu.HBM) for v in operands[kept:]]
    return pl.pallas_call(
        kernel,
        out_shape=tuple(outs),
        in_specs=[SMEM] + [VMEM] * len(held) + [pl.BlockSpec(memory_space=space)] * loads,
        out_specs=out_specs or [VMEM] * len(outs),
        scratch_shapes=list(scratch),
        compiler_params=pltpu.CompilerParams(vmem_limit_bytes=20 * 2**20),
        cost_estimate=pl.CostEstimate(
            flops=int(micros * 1e7), transcendentals=0, bytes_accessed=int(micros * 3e4)
        ),
        name=name,
    )(operands[0], *held, *far)


def positions(n):
    return (
        lax.broadcasted_iota(jnp.int32, (n, n), 0),
        lax.broadcasted_iota(jnp.int32, (n, n), 1),
    )


def halved(square):
    row, col = positions(square.shape[0])
    return jnp.where(row > col, square, jnp.where(row == col, 0.5 * square, 0.0))


def three(a):
    hi = a.astype(BF16)
    rest = a - hi.astype(F32)
    mid = rest.astype(BF16)
    return hi, mid, (rest - mid.astype(F32)).astype(BF16)


def dot3f(a, b, dims=NN):
    return dot3(split(a), split(b), dims)


def block_inverses(factor, size):
    n = factor.shape[0]
    row, col = positions(n)
    same = (row // size) == (col // size)
    lower = jnp.where(same & (row >= col), factor, 0.0)
    packed = lower[:size]
    for k in range(1, n // size):
        packed = packed + lower[k * size : (k + 1) * size]
    line = lax.broadcasted_iota(jnp.int32, (size, n), 0)
    lane = lax.broadcasted_iota(jnp.int32, (size, n), 1) % size
    columns = jnp.concatenate([jnp.where(lane == j, packed, 0.0) for j in range(size)], axis=0)
    ones = jnp.where(same, 1.0, 0.0).astype(BF16)
    hi, mid, lo = three(columns)
    spread = one(hi, ones) + (one(mid, ones) + one(lo, ones))
    x = jnp.where(line == lane, 1.0, 0.0)
    for j in range(size):
        column = spread[j * size : (j + 1) * size]
        solved = x[j : j + 1] / column[j : j + 1]
        x = jnp.where(line == j, solved, x - jnp.where(line > j, column, 0.0) * solved)
    return jnp.where(same, jnp.concatenate([x] * (n // size), axis=0), 0.0)


def inverses_of(factors):
    n = factors[0].shape[0]
    half = n // 2
    size = 16
    xs = [block_inverses(f, size) for f in factors]
    blocks = [(f, x, at) for f, x in zip(factors, xs) for at in (0, half)]
    corners = [x[at : at + half, at : at + half] for f, x, at in blocks]
    belows = [f[at : at + half, at : at + half] for f, x, at in blocks]
    row, col = positions(half)
    while size < half:
        inside = (row // (2 * size) == col // (2 * size)) & (row // size > col // size)
        parts = [full(jnp.where(inside, f, 0.0), x) for f, x in zip(belows, corners)]
        corners = [x - full(x, p) for x, p in zip(corners, parts)]
        size *= 2
    outs = []
    parts = [full(f[half:, :half], corners[2 * k]) for k, f in enumerate(factors)]
    parts = [full(corners[2 * k + 1], p) for k, p in enumerate(parts)]
    for k, p in enumerate(parts):
        top = jnp.concatenate([corners[2 * k], jnp.zeros((half, half), F32)], axis=1)
        low = jnp.concatenate([-p, corners[2 * k + 1]], axis=1)
        outs.append(jnp.concatenate([top, low], axis=0))
    return outs


def inverse_kernel(place, *refs):
    count = (len(refs) - 5) // 2
    sources, (a2, a2t, a1, a1t), targets, sems = (
        refs[:count],
        refs[count : count + 4],
        refs[count + 4 : -1],
        refs[-1],
    )
    copies = [
        pltpu.make_async_copy(source, target, sems.at[k])
        for k, (source, target) in enumerate(zip(sources, targets))
    ]
    for copy in copies:
        copy.start()
    copies[0].wait()
    copies[1].wait()
    x2, x1 = inverses_of([targets[0][...], targets[1][...]])
    a2[...] = x2
    a1[...] = x1
    a2t[...] = x2.T
    a1t[...] = x1.T
    for copy in copies[2:]:
        copy.wait()


def weight_kernel(place, a2, a2t, a1, a1t, d2, d1, c, l2, l1, bl, d2t, d1t, vt, w_hi, w_lo, bl_hi, bl_lo):
    n = d2.shape[0]
    d2t[...] = d2[...].T
    d1t[...] = d1[...].T
    x1 = split(a1[...])
    x2 = split(a2[...])
    cs = split(c[...])
    vt[0, :, :n] = a2t[...]
    vt[0, :, n:] = jnp.zeros((n, n), F32)
    vt[1, :, :n] = -dot3(x2, split(dot3(cs, x1))).T
    vt[1, :, n:] = a1t[...]
    w1 = dot3(x1, split(l1[...]))
    hi, lo = split(w1)
    w_hi[n:] = hi
    w_lo[n:] = lo
    hi, lo = split(dot3(x2, split(l2[...] - dot3(cs, (hi, lo)))))
    w_hi[:n] = hi
    w_lo[:n] = lo
    bl_hi[...], bl_lo[...] = split(bl[...])


def first_kernel(place, g2, g1, p2, p1, along_x, along_y):
    w = g2.shape[0]
    along_x[:w] = g1[...]
    along_x[w : 2 * w] = p2[...]
    along_x[2 * w :] = p1[...]
    along_y[...] = g2[...]


def far_kernel(place, x0, y0, x1, x3, x2, y1, y3, y2, far_x, far_y):
    w = y0.shape[0]
    for k, (fx, fy) in enumerate(((x0, y0), (x1, y1), (x2, y2), (x3, y3))):
        far_x[k * w : (k + 1) * w] = fy[...]
        far_y[k * w : (k + 1) * w] = fx[:w]


def gram_kernel(
    place, x0, y0, x1, x3, x2, y1, y3, y2, dx1, dx3, dx2, dy1, dy3, dy2, hi, lo, keep, send, p,
):
    x, y, core = (place[0], place[1], place[2])
    n = hi.shape[0] // 2
    w = y0.shape[0]

    def put(values, half, xx, yy):
        at = pl.multiple_of(half * n + ((yy & 3) * 4 + (xx & 3)) * w, w)
        h, l = split(values)
        hi[pl.ds(at, w)] = h
        lo[pl.ds(at, w)] = l

    for k, (fx, fy) in enumerate(((x0, y0), (x1, y1), (x2, y2), (x3, y3))):
        put(fy[...], 0, x, y + 4 - k)
        put(fx[:w], 1, x + 4 - k, y)
        rows = pl.ds(pl.multiple_of(((x + 4 - k) & 3) * w, w), w)
        p[0, rows] = fx[w : 2 * w]
        p[1, rows] = fx[2 * w :]
    for k, (fx, fy) in enumerate(((dx1, dy1), (dx2, dy2), (dx3, dy3))):
        for j in range(4):
            rows = slice(j * w, (j + 1) * w)
            put(fx[rows], 0, x + 3 - k, y + 4 - j)
            put(fy[rows], 1, x + 4 - j, y + 3 - k)
    both = split(jnp.concatenate([p[0], p[1]], axis=0))
    wide = dot3((hi[:n], lo[:n]), both, NT)
    tall = dot3((hi[n:], lo[n:]), split(p[1]), NT)
    half = n // 2
    packed = jnp.concatenate([wide, jnp.concatenate([tall[:half], tall[half:]], axis=1)], axis=0)
    part = packed.shape[0] // 2

    @pl.when(core == 0)
    def _():
        keep[...] = packed[:part]
        send[...] = packed[part:]

    @pl.when(core == 1)
    def _():
        keep[...] = packed[part:]
        send[...] = packed[:part]


def add_kernel(place, a, b, out):
    out[...] = a[...] + b[...]


def stack_kernel(place, a, b, c, d, out):
    out[0] = a[...]
    out[1] = b[...]
    out[2] = c[...]
    out[3] = d[...]


def below_sum_kernel(place, hi, lo, bl_hi, bl_lo, a2t, a1t, c, keep, send):
    core = place[2]
    n = a2t.shape[0]
    share = n // 4
    below = (bl_hi[...], bl_lo[...])
    q2 = dot3((hi[:n], lo[:n]), below)
    u2 = dot3f(a2t[...], q2)
    q1 = dot3((hi[n:], lo[n:]), below)
    u1 = dot3f(a1t[...], q1 - dot3f(c[...].T, u2))
    for k in range(2):

        @pl.when(core == k)
        def _():
            for r in range(4):
                ref = keep if r % 2 == k else send
                ref[r // 2, :share] = u2[r * share : (r + 1) * share]
                ref[r // 2, share:] = u1[r * share : (r + 1) * share]


def pair_kernel(place, keep, got, mine, send):
    z = place[3]
    mine[...] = (keep[pl.ds(z, 1)] + got[pl.ds(z, 1)])[0]
    send[...] = (keep[pl.ds(1 - z, 1)] + got[pl.ds(1 - z, 1)])[0]


def below_kernel(place, hi, lo, w_hi, w_lo, vt, grad, out, s2t, s1t, held, sems):
    w = s2t.shape[0]
    weights = (w_hi[...], w_lo[...])
    steps = sems.shape[0]
    tall = held.shape[0] // steps
    copies = []
    for k in range(steps):
        rows = pl.ds(k * tall, tall)
        held[rows] = grad[rows] - dot3((hi[:, rows], lo[:, rows]), weights, TN)
        copies.append(pltpu.make_async_copy(held.at[rows], out.at[rows], sems.at[k]))
        copies[-1].start()
    at = pl.multiple_of((place[1] * 4 + place[0]) * w, w)
    v = jnp.concatenate([vt[0, pl.ds(at, w)], vt[1, pl.ds(at, w)]], axis=0)
    solved = dot3(split(v), (hi[...], lo[...]))
    s2t[...] = solved[:w]
    s1t[...] = solved[w:]
    for copy in copies:
        copy.wait()


def chain_kernel(
    place, mine, other, a2, a2t, a1, a1t, d2t, d1t, c, gd2, gd1, gc, l2, l1, gl2, gl1,
    left2, left1, o_diag2, o_diag1, o_cross, whole, tall, rows2, rows1, rowsx, rowsxt,
):
    n = a2.shape[0]
    first = place[2] == 0
    quarter = n // 4
    half = n // 2
    for k, by in enumerate((0, 1, 3, 2)):
        y = (place[1] + 4 - by) & 3
        a, b = (mine[k], other[k])
        block = jnp.concatenate([jnp.where(first, a, b), jnp.where(first, b, a)], axis=0)
        whole[y] = block[:n]
        tall[y, :half] = block[n:, :quarter]
        tall[y, half:] = block[n:, quarter:]
    row, col = positions(n)
    lower = row >= col
    both = [dot3f(a2t[...], whole[y]) for y in range(4)]
    gram2 = jnp.concatenate([b[:, :quarter] for b in both], axis=1)
    gram_cross = jnp.concatenate([b[:, quarter:] for b in both], axis=1)
    tall = jnp.concatenate([tall[y] for y in range(4)], axis=1)
    below = dot3f(a1t[...], tall - dot3f(c[...].T, gram_cross))
    inner = halved(dot3f(d2t[...], gd2[...] - jnp.where(lower, gram2, 0.0)))
    spread = dot3f(dot3f(a2t[...], inner), a2[...])
    sym2 = spread + spread.T
    rows2[...] = sym2
    o_diag2[...] = halved(sym2)
    cross = dot3f(gc[...] - gram_cross - dot3f(sym2, c[...]), a1[...])
    o_cross[...] = cross
    rowsx[...] = cross
    cross_turned = cross.T
    rowsxt[...] = cross_turned
    gram1 = dot3f(cross_turned, c[...]) + below
    inner = halved(dot3f(d1t[...], gd1[...] - jnp.where(lower, gram1, 0.0)))
    spread = dot3f(dot3f(a1t[...], inner), a1[...])
    sym1 = spread + spread.T
    rows1[...] = sym1
    o_diag1[...] = halved(sym1)
    share = gl2.shape[0]
    at = pl.ds(pl.multiple_of((place[3] * 2 + place[2]) * share, share), share)
    l2s, l1s = (split(l2[...]), split(l1[...]))
    left2[...] = gl2[...] - dot3(split(rows2[at]), l2s) - dot3(split(rowsx[at]), l1s)
    left1[...] = gl1[...] - dot3(split(rowsxt[at]), l2s) - dot3(split(rows1[at]), l1s)


def left_kernel(place, left2, left1, part, got, o_left2, o_left1):
    share = left2.shape[0]
    o_left2[...] = left2[...] - (part[:share] + got[:share])
    o_left1[...] = left1[...] - (part[share:] + got[share:])


def shifted(value, axis, by):
    count = lax.axis_size(axis)
    return lax.ppermute(value, axis, [(i, (i + by) % count) for i in range(count)])


def shifts(value, axis):
    return [shifted(value, axis, k) for k in (1, 3, 2)]


def after(values, first):
    return lax.optimization_barrier((tuple(values), first))[0]


def body(d2, d1, c, l2, l1, bl, p2, p1, gd2, gd1, gc, gl2, gl1, gb, g2, g1):
    n = d2.shape[0]
    width = l2.shape[1]
    rows, w = p2.shape
    core = lax.axis_index("core")
    place = jnp.stack(
        [lax.axis_index("x"), lax.axis_index("y"), core, lax.axis_index("zlo")]
    ).astype(jnp.int32)
    along_x, along_y = call(
        first_kernel,
        "first",
        (near(3 * w, rows), near(w, rows)),
        (place, g2.T, g1.T, p2.T, p1.T),
        (),
        1.0,
        4,
    )
    xs = shifts(along_x, "x")
    ys = shifts(along_y, "y")
    square = near(n, n)
    given = after((d2, d1, c, l2, l1, bl, gd2, gd1, gc, gl2, gl1, gb), along_x)
    a2, a2t, a1, a1t, d2, d1, c, l2, l1, bl, gd2, gd1, gc, gl2, gl1, gb = call(
        inverse_kernel,
        "inverses",
        (square,) * 4 + tuple(near(*v.shape) for v in given),
        (place, *given),
        (pltpu.SemaphoreType.DMA((len(given),)),),
        4.0,
        len(given),
        pltpu.HBM,
    )
    pieces = (along_x, along_y, *xs, *ys)
    (x0,) = after((along_x,), a2)
    far_x, far_y = call(
        far_kernel, "far", (near(4 * w, rows),) * 2, (place, x0, *pieces[1:]), (), 0.6
    )
    dxs = [shifted(far_x, "x", k) for k in (1, 3)]
    dys = [shifted(far_y, "y", k) for k in (1, 3)]
    halves = (near(rows, width, dtype=BF16),) * 2
    thick = (near(2 * n, width, dtype=BF16),) * 2
    d2t, d1t, vt, w_hi, w_lo, bl_hi, bl_lo = call(
        weight_kernel,
        "weights",
        (square, square, near(2, n, 2 * n), *thick, *halves),
        (place, a2, a2t, a1, a1t, d2, d1, c, l2, l1, bl),
        (),
        2.7,
    )
    dxs.append(shifted(after(dxs[:1], w_hi)[0], "x", 1))
    dys.append(shifted(after(dys[1:2], w_hi)[0], "y", 3))
    half = near(6 * n // 8, n // 2)
    (x0,) = after((along_x,), w_hi)
    hi, lo, keep, send = call(
        gram_kernel,
        "grams",
        (near(2 * n, rows, dtype=BF16),) * 2 + (half, half),
        (place, x0, *pieces[1:], *dxs, *dys),
        (pltpu.VMEM((2, 4 * w, rows), F32),),
        2.0,
    )
    (gram,) = call(
        add_kernel, "pair_gram", (half,), (place, keep, shifted(send, "core", 1)), (), 0.5
    )
    (below_hi,) = after((bl_hi,), gram)
    keep, send = call(
        below_sum_kernel,
        "below_sums",
        (near(2, n // 2, width),) * 2,
        (place, hi, lo, below_hi, bl_lo, a2t, a1t, c),
        (),
        3.0,
    )
    (gram,) = call(
        add_kernel,
        "row_gram",
        (half,),
        (place, *after((gram,), keep), shifted(gram, "zlo", 1)),
        (),
        0.6,
    )
    (send,) = after((send,), gram)
    part, send = call(
        pair_kernel,
        "pair_sums",
        (near(n // 2, width),) * 2,
        (place, keep, shifted(send, "core", 1)),
        (),
        0.6,
    )
    got = shifted(send, "zlo", 1)
    (gb,) = after((gb,), (send, gram))
    out_below, s2t, s1t = call(
        below_kernel,
        "below_outputs",
        (shaped(rows, width), shaped(w, rows), shaped(w, rows)),
        (place, hi, lo, w_hi, w_lo, vt, gb),
        (pltpu.VMEM(gb.shape, F32), pltpu.SemaphoreType.DMA((4,))),
        3.8,
        out_specs=[pl.BlockSpec(memory_space=pltpu.HBM), VMEM, VMEM],
    )
    (mine,) = call(
        stack_kernel,
        "stack",
        (near(4, *half.shape),),
        (place, *after((gram,), s2t), *shifts(gram, "y")),
        (),
        0.8,
    )
    left2, left1, diag2, diag1, cross = call(
        chain_kernel,
        "chain",
        (near(*gl2.shape), near(*gl2.shape), shaped(n, n), shaped(n, n), shaped(n, n)),
        (place, mine, shifted(mine, "core", 1), a2, a2t, a1, a1t, d2t, d1t, c, gd2, gd1, gc, l2, l1, gl2, gl1),
        (pltpu.VMEM((4, n, n // 2), F32), pltpu.VMEM((4, n, n // 4), F32))
        + (pltpu.VMEM((n, n), F32),) * 4,
        5.2,
    )
    left2, left1 = call(
        left_kernel, "left", (shaped(*gl2.shape),) * 2, (place, left2, left1, part, got), (), 1.0
    )
    return out_below, left2, left1, diag2, diag1, cross, s2t.T, s1t.T


def solution(mesh):
    fine = Mesh(
        mesh.devices.reshape(2, 2, 4, 4, 4), ("zlo", "core", "y", "x", "dep")
    )
    row, col, deep = (("zlo", "core"), ("y", "x"), ("y", "x", "dep"))
    return jax.shard_map(
        body,
        mesh=fine,
        in_specs=(
            P(),
            P(),
            P(),
            P(None, deep),
            P(None, deep),
            P(row, deep),
            P(row, col),
            P(row, col),
            P(),
            P(),
            P(),
            P(row, deep),
            P(row, deep),
            P(row, deep),
            P(row, col),
            P(row, col),
        ),
        out_specs=(
            P(row, deep),
            P(row, deep),
            P(row, deep),
            P(),
            P(),
            P(),
            P(row, col),
            P(row, col),
        ),
        check_vma=False,
    )
```

```python
import jax
import jax.numpy as jnp
from jax import lax
from jax.experimental import pallas as pl
from jax.experimental.pallas import tpu as pltpu
from jax.sharding import Mesh, PartitionSpec as P

F32 = jnp.float32
BF16 = jnp.bfloat16
VMEM = pl.BlockSpec(memory_space=pltpu.VMEM)
SMEM = pl.BlockSpec(memory_space=pltpu.SMEM)
NN = (((1,), (0,)), ((), ()))
NT = (((1,), (1,)), ((), ()))
TN = (((0,), (0,)), ((), ()))


def full(a, b, dims=NN):
    return lax.dot_general(a, b, dims, precision=lax.Precision.HIGHEST, preferred_element_type=F32)


def one(a, b, dims=NN):
    return lax.dot_general(a, b, dims, preferred_element_type=F32)


def split(a):
    hi = a.astype(BF16)
    return hi, (a - hi.astype(F32)).astype(BF16)


def dot3(a, b, dims=NN):
    return one(a[0], b[0], dims) + (one(a[0], b[1], dims) + one(a[1], b[0], dims))


def shaped(*shape, dtype=F32):
    return jax.ShapeDtypeStruct(shape, dtype)


def near(*shape, dtype=F32):
    return pltpu.VMEM(shape, dtype)


def call(kernel, name, outs, operands, scratch=(), micros=2.0, loads=0, space=pltpu.VMEM, out_specs=None):
    kept = len(operands) - loads
    held = [pltpu.with_memory_space_constraint(v, pltpu.VMEM) for v in operands[1:kept]]
    far = [pltpu.with_memory_space_constraint(v, pltpu.HBM) for v in operands[kept:]]
    return pl.pallas_call(
        kernel,
        out_shape=tuple(outs),
        in_specs=[SMEM] + [VMEM] * len(held) + [pl.BlockSpec(memory_space=space)] * loads,
        out_specs=out_specs or [VMEM] * len(outs),
        scratch_shapes=list(scratch),
        compiler_params=pltpu.CompilerParams(vmem_limit_bytes=20 * 2**20),
        cost_estimate=pl.CostEstimate(
            flops=int(micros * 1e9), transcendentals=0, bytes_accessed=int(micros * 3e6)
        ),
        name=name,
    )(operands[0], *held, *far)


def positions(n):
    return (
        lax.broadcasted_iota(jnp.int32, (n, n), 0),
        lax.broadcasted_iota(jnp.int32, (n, n), 1),
    )


def halved(square):
    row, col = positions(square.shape[0])
    return jnp.where(row > col, square, jnp.where(row == col, 0.5 * square, 0.0))


def three(a):
    hi = a.astype(BF16)
    rest = a - hi.astype(F32)
    mid = rest.astype(BF16)
    return hi, mid, (rest - mid.astype(F32)).astype(BF16)


def dot3f(a, b, dims=NN):
    return dot3(split(a), split(b), dims)


def block_inverses(factor, size):
    n = factor.shape[0]
    row, col = positions(n)
    same = (row // size) == (col // size)
    lower = jnp.where(same & (row >= col), factor, 0.0)
    packed = lower[:size]
    for k in range(1, n // size):
        packed = packed + lower[k * size : (k + 1) * size]
    line = lax.broadcasted_iota(jnp.int32, (size, n), 0)
    lane = lax.broadcasted_iota(jnp.int32, (size, n), 1) % size
    columns = jnp.concatenate([jnp.where(lane == j, packed, 0.0) for j in range(size)], axis=0)
    ones = jnp.where(same, 1.0, 0.0).astype(BF16)
    hi, mid, lo = three(columns)
    spread = one(hi, ones) + (one(mid, ones) + one(lo, ones))
    x = jnp.where(line == lane, 1.0, 0.0)
    for j in range(size):
        column = spread[j * size : (j + 1) * size]
        solved = x[j : j + 1] / column[j : j + 1]
        x = jnp.where(line == j, solved, x - jnp.where(line > j, column, 0.0) * solved)
    return jnp.where(same, jnp.concatenate([x] * (n // size), axis=0), 0.0)


def inverses_of(factors):
    n = factors[0].shape[0]
    half = n // 2
    size = 16
    xs = [block_inverses(f, size) for f in factors]
    blocks = [(f, x, at) for f, x in zip(factors, xs) for at in (0, half)]
    corners = [x[at : at + half, at : at + half] for f, x, at in blocks]
    belows = [f[at : at + half, at : at + half] for f, x, at in blocks]
    row, col = positions(half)
    while size < half:
        inside = (row // (2 * size) == col // (2 * size)) & (row // size > col // size)
        parts = [full(jnp.where(inside, f, 0.0), x) for f, x in zip(belows, corners)]
        corners = [x - full(x, p) for x, p in zip(corners, parts)]
        size *= 2
    outs = []
    parts = [full(f[half:, :half], corners[2 * k]) for k, f in enumerate(factors)]
    parts = [full(corners[2 * k + 1], p) for k, p in enumerate(parts)]
    for k, p in enumerate(parts):
        top = jnp.concatenate([corners[2 * k], jnp.zeros((half, half), F32)], axis=1)
        low = jnp.concatenate([-p, corners[2 * k + 1]], axis=1)
        outs.append(jnp.concatenate([top, low], axis=0))
    return outs


def inverse_kernel(place, *refs):
    count = (len(refs) - 5) // 2
    sources, (a2, a2t, a1, a1t), targets, sems = (
        refs[:count],
        refs[count : count + 4],
        refs[count + 4 : -1],
        refs[-1],
    )
    copies = [
        pltpu.make_async_copy(source, target, sems.at[k])
        for k, (source, target) in enumerate(zip(sources, targets))
    ]
    for copy in copies:
        copy.start()
    copies[0].wait()
    copies[1].wait()
    x2, x1 = inverses_of([targets[0][...], targets[1][...]])
    a2[...] = x2
    a1[...] = x1
    a2t[...] = x2.T
    a1t[...] = x1.T
    for copy in copies[2:]:
        copy.wait()


def weight_kernel(place, a2, a2t, a1, a1t, d2, d1, c, l2, l1, bl, d2t, d1t, vt, w_hi, w_lo, bl_hi, bl_lo):
    n = d2.shape[0]
    d2t[...] = d2[...].T
    d1t[...] = d1[...].T
    x1 = split(a1[...])
    x2 = split(a2[...])
    cs = split(c[...])
    vt[0, :, :n] = a2t[...]
    vt[0, :, n:] = jnp.zeros((n, n), F32)
    vt[1, :, :n] = -dot3(x2, split(dot3(cs, x1))).T
    vt[1, :, n:] = a1t[...]
    w1 = dot3(x1, split(l1[...]))
    hi, lo = split(w1)
    w_hi[n:] = hi
    w_lo[n:] = lo
    hi, lo = split(dot3(x2, split(l2[...] - dot3(cs, (hi, lo)))))
    w_hi[:n] = hi
    w_lo[:n] = lo
    bl_hi[...], bl_lo[...] = split(bl[...])


def first_kernel(place, g2, g1, p2, p1, along_x, along_y):
    w = g2.shape[0]
    along_x[:w] = g1[...]
    along_x[w : 2 * w] = p2[...]
    along_x[2 * w :] = p1[...]
    along_y[...] = g2[...]


def far_kernel(place, x0, y0, x1, x3, x2, y1, y3, y2, far_x, far_y):
    w = y0.shape[0]
    for k, (fx, fy) in enumerate(((x0, y0), (x1, y1), (x2, y2), (x3, y3))):
        far_x[k * w : (k + 1) * w] = fy[...]
        far_y[k * w : (k + 1) * w] = fx[:w]


def gram_kernel(
    place, x0, y0, x1, x3, x2, y1, y3, y2, dx1, dx3, dx2, dy1, dy3, dy2, hi, lo, keep, send, p,
):
    x, y, core = (place[0], place[1], place[2])
    n = hi.shape[0] // 2
    w = y0.shape[0]

    def put(values, half, xx, yy):
        at = pl.multiple_of(half * n + ((yy & 3) * 4 + (xx & 3)) * w, w)
        h, l = split(values)
        hi[pl.ds(at, w)] = h
        lo[pl.ds(at, w)] = l

    for k, (fx, fy) in enumerate(((x0, y0), (x1, y1), (x2, y2), (x3, y3))):
        put(fy[...], 0, x, y + 4 - k)
        put(fx[:w], 1, x + 4 - k, y)
        rows = pl.ds(pl.multiple_of(((x + 4 - k) & 3) * w, w), w)
        p[0, rows] = fx[w : 2 * w]
        p[1, rows] = fx[2 * w :]
    for k, (fx, fy) in enumerate(((dx1, dy1), (dx2, dy2), (dx3, dy3))):
        for j in range(4):
            rows = slice(j * w, (j + 1) * w)
            put(fx[rows], 0, x + 3 - k, y + 4 - j)
            put(fy[rows], 1, x + 4 - j, y + 3 - k)
    both = split(jnp.concatenate([p[0], p[1]], axis=0))
    wide = dot3((hi[:n], lo[:n]), both, NT)
    tall = dot3((hi[n:], lo[n:]), split(p[1]), NT)
    half = n // 2
    packed = jnp.concatenate([wide, jnp.concatenate([tall[:half], tall[half:]], axis=1)], axis=0)
    part = packed.shape[0] // 2

    @pl.when(core == 0)
    def _():
        keep[...] = packed[:part]
        send[...] = packed[part:]

    @pl.when(core == 1)
    def _():
        keep[...] = packed[part:]
        send[...] = packed[:part]


def add_kernel(place, a, b, out):
    out[...] = a[...] + b[...]


def stack_kernel(place, a, b, c, d, out):
    out[0] = a[...]
    out[1] = b[...]
    out[2] = c[...]
    out[3] = d[...]


def below_sum_kernel(place, hi, lo, bl_hi, bl_lo, a2t, a1t, c, keep, send):
    core = place[2]
    n = a2t.shape[0]
    share = n // 4
    below = (bl_hi[...], bl_lo[...])
    q2 = dot3((hi[:n], lo[:n]), below)
    u2 = dot3f(a2t[...], q2)
    q1 = dot3((hi[n:], lo[n:]), below)
    u1 = dot3f(a1t[...], q1 - dot3f(c[...].T, u2))
    for k in range(2):

        @pl.when(core == k)
        def _():
            for r in range(4):
                ref = keep if r % 2 == k else send
                ref[r // 2, :share] = u2[r * share : (r + 1) * share]
                ref[r // 2, share:] = u1[r * share : (r + 1) * share]


def pair_kernel(place, keep, got, mine, send):
    z = place[3]
    mine[...] = (keep[pl.ds(z, 1)] + got[pl.ds(z, 1)])[0]
    send[...] = (keep[pl.ds(1 - z, 1)] + got[pl.ds(1 - z, 1)])[0]


def below_kernel(place, hi, lo, w_hi, w_lo, vt, grad, out, s2t, s1t, held, sems):
    w = s2t.shape[0]
    weights = (w_hi[...], w_lo[...])
    steps = sems.shape[0]
    tall = held.shape[0] // steps
    copies = []
    for k in range(steps):
        rows = pl.ds(k * tall, tall)
        held[rows] = grad[rows] - dot3((hi[:, rows], lo[:, rows]), weights, TN)
        copies.append(pltpu.make_async_copy(held.at[rows], out.at[rows], sems.at[k]))
        copies[-1].start()
    at = pl.multiple_of((place[1] * 4 + place[0]) * w, w)
    v = jnp.concatenate([vt[0, pl.ds(at, w)], vt[1, pl.ds(at, w)]], axis=0)
    solved = dot3(split(v), (hi[...], lo[...]))
    s2t[...] = solved[:w]
    s1t[...] = solved[w:]
    for copy in copies:
        copy.wait()


def chain_kernel(
    place, mine, other, a2, a2t, a1, a1t, d2t, d1t, c, gd2, gd1, gc, l2, l1, gl2, gl1,
    left2, left1, o_diag2, o_diag1, o_cross, whole, tall, rows2, rows1, rowsx, rowsxt,
):
    n = a2.shape[0]
    first = place[2] == 0
    quarter = n // 4
    half = n // 2
    for k, by in enumerate((0, 1, 3, 2)):
        y = (place[1] + 4 - by) & 3
        a, b = (mine[k], other[k])
        block = jnp.concatenate([jnp.where(first, a, b), jnp.where(first, b, a)], axis=0)
        whole[y] = block[:n]
        tall[y, :half] = block[n:, :quarter]
        tall[y, half:] = block[n:, quarter:]
    row, col = positions(n)
    lower = row >= col
    both = [dot3f(a2t[...], whole[y]) for y in range(4)]
    gram2 = jnp.concatenate([b[:, :quarter] for b in both], axis=1)
    gram_cross = jnp.concatenate([b[:, quarter:] for b in both], axis=1)
    tall = jnp.concatenate([tall[y] for y in range(4)], axis=1)
    below = dot3f(a1t[...], tall - dot3f(c[...].T, gram_cross))
    inner = halved(dot3f(d2t[...], gd2[...] - jnp.where(lower, gram2, 0.0)))
    spread = dot3f(dot3f(a2t[...], inner), a2[...])
    sym2 = spread + spread.T
    rows2[...] = sym2
    o_diag2[...] = halved(sym2)
    cross = dot3f(gc[...] - gram_cross - dot3f(sym2, c[...]), a1[...])
    o_cross[...] = cross
    rowsx[...] = cross
    cross_turned = cross.T
    rowsxt[...] = cross_turned
    gram1 = dot3f(cross_turned, c[...]) + below
    inner = halved(dot3f(d1t[...], gd1[...] - jnp.where(lower, gram1, 0.0)))
    spread = dot3f(dot3f(a1t[...], inner), a1[...])
    sym1 = spread + spread.T
    rows1[...] = sym1
    o_diag1[...] = halved(sym1)
    share = gl2.shape[0]
    at = pl.ds(pl.multiple_of((place[3] * 2 + place[2]) * share, share), share)
    l2s, l1s = (split(l2[...]), split(l1[...]))
    left2[...] = gl2[...] - dot3(split(rows2[at]), l2s) - dot3(split(rowsx[at]), l1s)
    left1[...] = gl1[...] - dot3(split(rowsxt[at]), l2s) - dot3(split(rows1[at]), l1s)


def left_kernel(place, left2, left1, part, got, o_left2, o_left1):
    share = left2.shape[0]
    o_left2[...] = left2[...] - (part[:share] + got[:share])
    o_left1[...] = left1[...] - (part[share:] + got[share:])


def shifted(value, axis, by):
    count = lax.axis_size(axis)
    return lax.ppermute(value, axis, [(i, (i + by) % count) for i in range(count)])


def shifts(value, axis):
    return [shifted(value, axis, k) for k in (1, 3, 2)]


def after(values, first):
    return lax.optimization_barrier((tuple(values), first))[0]


def body(d2, d1, c, l2, l1, bl, p2, p1, gd2, gd1, gc, gl2, gl1, gb, g2, g1):
    n = d2.shape[0]
    width = l2.shape[1]
    rows, w = p2.shape
    core = lax.axis_index("core")
    place = jnp.stack(
        [lax.axis_index("x"), lax.axis_index("y"), core, lax.axis_index("zlo")]
    ).astype(jnp.int32)
    along_x, along_y = call(
        first_kernel,
        "first",
        (near(3 * w, rows), near(w, rows)),
        (place, g2.T, g1.T, p2.T, p1.T),
        (),
        1.0,
        4,
    )
    xs = shifts(along_x, "x")
    ys = shifts(along_y, "y")
    square = near(n, n)
    given = after((d2, d1, c, l2, l1, bl, gd2, gd1, gc, gl2, gl1, gb), along_x)
    a2, a2t, a1, a1t, d2, d1, c, l2, l1, bl, gd2, gd1, gc, gl2, gl1, gb = call(
        inverse_kernel,
        "inverses",
        (square,) * 4 + tuple(near(*v.shape) for v in given),
        (place, *given),
        (pltpu.SemaphoreType.DMA((len(given),)),),
        4.0,
        len(given),
        pltpu.HBM,
    )
    pieces = (along_x, along_y, *xs, *ys)
    (x0,) = after((along_x,), a2)
    far_x, far_y = call(
        far_kernel, "far", (near(4 * w, rows),) * 2, (place, x0, *pieces[1:]), (), 0.6
    )
    dxs = [shifted(far_x, "x", k) for k in (1, 3)]
    dys = [shifted(far_y, "y", k) for k in (1, 3)]
    halves = (near(rows, width, dtype=BF16),) * 2
    thick = (near(2 * n, width, dtype=BF16),) * 2
    d2t, d1t, vt, w_hi, w_lo, bl_hi, bl_lo = call(
        weight_kernel,
        "weights",
        (square, square, near(2, n, 2 * n), *thick, *halves),
        (place, a2, a2t, a1, a1t, d2, d1, c, l2, l1, bl),
        (),
        2.7,
    )
    dxs.append(shifted(dxs[0], "x", 1))
    dys.append(shifted(dys[1], "y", 3))
    half = near(6 * n // 8, n // 2)
    (x0,) = after((along_x,), w_hi)
    hi, lo, keep, send = call(
        gram_kernel,
        "grams",
        (near(2 * n, rows, dtype=BF16),) * 2 + (half, half),
        (place, x0, *pieces[1:], *dxs, *dys),
        (pltpu.VMEM((2, 4 * w, rows), F32),),
        2.0,
    )
    (gram,) = call(
        add_kernel, "pair_gram", (half,), (place, keep, shifted(send, "core", 1)), (), 0.5
    )
    (below_hi,) = after((bl_hi,), gram)
    keep, send = call(
        below_sum_kernel,
        "below_sums",
        (near(2, n // 2, width),) * 2,
        (place, hi, lo, below_hi, bl_lo, a2t, a1t, c),
        (),
        3.0,
    )
    (gram,) = call(
        add_kernel,
        "row_gram",
        (half,),
        (place, *after((gram,), keep), shifted(gram, "zlo", 1)),
        (),
        0.6,
    )
    (send,) = after((send,), gram)
    part, send = call(
        pair_kernel,
        "pair_sums",
        (near(n // 2, width),) * 2,
        (place, keep, shifted(send, "core", 1)),
        (),
        0.6,
    )
    got = shifted(send, "zlo", 1)
    (gb,) = after((gb,), (send, gram))
    out_below, s2t, s1t = call(
        below_kernel,
        "below_outputs",
        (shaped(rows, width), shaped(w, rows), shaped(w, rows)),
        (place, hi, lo, w_hi, w_lo, vt, gb),
        (pltpu.VMEM(gb.shape, F32), pltpu.SemaphoreType.DMA((4,))),
        3.8,
        out_specs=[pl.BlockSpec(memory_space=pltpu.HBM), VMEM, VMEM],
    )
    (mine,) = call(
        stack_kernel,
        "stack",
        (near(4, *half.shape),),
        (place, *after((gram,), s2t), *shifts(gram, "y")),
        (),
        0.8,
    )
    left2, left1, diag2, diag1, cross = call(
        chain_kernel,
        "chain",
        (near(*gl2.shape), near(*gl2.shape), shaped(n, n), shaped(n, n), shaped(n, n)),
        (place, mine, shifted(mine, "core", 1), a2, a2t, a1, a1t, d2t, d1t, c, gd2, gd1, gc, l2, l1, gl2, gl1),
        (pltpu.VMEM((4, n, n // 2), F32), pltpu.VMEM((4, n, n // 4), F32))
        + (pltpu.VMEM((n, n), F32),) * 4,
        5.2,
    )
    left2, left1 = call(
        left_kernel, "left", (shaped(*gl2.shape),) * 2, (place, left2, left1, part, got), (), 1.0
    )
    return out_below, left2, left1, diag2, diag1, cross, s2t.T, s1t.T


def solution(mesh):
    fine = Mesh(
        mesh.devices.reshape(2, 2, 4, 4, 4), ("zlo", "core", "y", "x", "dep")
    )
    row, col, deep = (("zlo", "core"), ("y", "x"), ("y", "x", "dep"))
    return jax.shard_map(
        body,
        mesh=fine,
        in_specs=(
            P(),
            P(),
            P(),
            P(None, deep),
            P(None, deep),
            P(row, deep),
            P(row, col),
            P(row, col),
            P(),
            P(),
            P(),
            P(row, deep),
            P(row, deep),
            P(row, deep),
            P(row, col),
            P(row, col),
        ),
        out_specs=(
            P(row, deep),
            P(row, deep),
            P(row, deep),
            P(),
            P(),
            P(),
            P(row, col),
            P(row, col),
        ),
        check_vma=False,
    )
```

```python
import jax
import jax.numpy as jnp
from jax import lax
from jax.experimental import pallas as pl
from jax.experimental.pallas import tpu as pltpu
from jax.sharding import Mesh, PartitionSpec as P

F32 = jnp.float32
BF16 = jnp.bfloat16
VMEM = pl.BlockSpec(memory_space=pltpu.VMEM)
SMEM = pl.BlockSpec(memory_space=pltpu.SMEM)
NN = (((1,), (0,)), ((), ()))
NT = (((1,), (1,)), ((), ()))
TN = (((0,), (0,)), ((), ()))


def full(a, b, dims=NN):
    return lax.dot_general(a, b, dims, precision=lax.Precision.HIGHEST, preferred_element_type=F32)


def one(a, b, dims=NN):
    return lax.dot_general(a, b, dims, preferred_element_type=F32)


def split(a):
    hi = a.astype(BF16)
    return hi, (a - hi.astype(F32)).astype(BF16)


def dot3(a, b, dims=NN):
    return one(a[0], b[0], dims) + (one(a[0], b[1], dims) + one(a[1], b[0], dims))


def shaped(*shape, dtype=F32):
    return jax.ShapeDtypeStruct(shape, dtype)


def near(*shape, dtype=F32):
    return pltpu.VMEM(shape, dtype)


def call(kernel, name, outs, operands, scratch=(), micros=2.0, loads=0, space=pltpu.VMEM, out_specs=None):
    kept = len(operands) - loads
    held = [pltpu.with_memory_space_constraint(v, pltpu.VMEM) for v in operands[1:kept]]
    far = [pltpu.with_memory_space_constraint(v, pltpu.HBM) for v in operands[kept:]]
    return pl.pallas_call(
        kernel,
        out_shape=tuple(outs),
        in_specs=[SMEM] + [VMEM] * len(held) + [pl.BlockSpec(memory_space=space)] * loads,
        out_specs=out_specs or [VMEM] * len(outs),
        scratch_shapes=list(scratch),
        compiler_params=pltpu.CompilerParams(vmem_limit_bytes=20 * 2**20),
        cost_estimate=pl.CostEstimate(
            flops=int(micros * 1e9), transcendentals=0, bytes_accessed=int(micros * 3e6)
        ),
        name=name,
    )(operands[0], *held, *far)


def positions(n):
    return (
        lax.broadcasted_iota(jnp.int32, (n, n), 0),
        lax.broadcasted_iota(jnp.int32, (n, n), 1),
    )


def halved(square):
    row, col = positions(square.shape[0])
    return jnp.where(row > col, square, jnp.where(row == col, 0.5 * square, 0.0))


def three(a):
    hi = a.astype(BF16)
    rest = a - hi.astype(F32)
    mid = rest.astype(BF16)
    return hi, mid, (rest - mid.astype(F32)).astype(BF16)


def dot3f(a, b, dims=NN):
    return dot3(split(a), split(b), dims)


def block_inverses(factor, size):
    n = factor.shape[0]
    row, col = positions(n)
    same = (row // size) == (col // size)
    lower = jnp.where(same & (row >= col), factor, 0.0)
    packed = lower[:size]
    for k in range(1, n // size):
        packed = packed + lower[k * size : (k + 1) * size]
    line = lax.broadcasted_iota(jnp.int32, (size, n), 0)
    lane = lax.broadcasted_iota(jnp.int32, (size, n), 1) % size
    columns = jnp.concatenate([jnp.where(lane == j, packed, 0.0) for j in range(size)], axis=0)
    ones = jnp.where(same, 1.0, 0.0).astype(BF16)
    hi, mid, lo = three(columns)
    spread = one(hi, ones) + (one(mid, ones) + one(lo, ones))
    x = jnp.where(line == lane, 1.0, 0.0)
    for j in range(size):
        column = spread[j * size : (j + 1) * size]
        solved = x[j : j + 1] / column[j : j + 1]
        x = jnp.where(line == j, solved, x - jnp.where(line > j, column, 0.0) * solved)
    return jnp.where(same, jnp.concatenate([x] * (n // size), axis=0), 0.0)


def inverses_of(factors):
    n = factors[0].shape[0]
    half = n // 2
    size = 16
    xs = [block_inverses(f, size) for f in factors]
    blocks = [(f, x, at) for f, x in zip(factors, xs) for at in (0, half)]
    corners = [x[at : at + half, at : at + half] for f, x, at in blocks]
    belows = [f[at : at + half, at : at + half] for f, x, at in blocks]
    row, col = positions(half)
    while size < half:
        inside = (row // (2 * size) == col // (2 * size)) & (row // size > col // size)
        parts = [full(jnp.where(inside, f, 0.0), x) for f, x in zip(belows, corners)]
        corners = [x - full(x, p) for x, p in zip(corners, parts)]
        size *= 2
    outs = []
    parts = [full(f[half:, :half], corners[2 * k]) for k, f in enumerate(factors)]
    parts = [full(corners[2 * k + 1], p) for k, p in enumerate(parts)]
    for k, p in enumerate(parts):
        top = jnp.concatenate([corners[2 * k], jnp.zeros((half, half), F32)], axis=1)
        low = jnp.concatenate([-p, corners[2 * k + 1]], axis=1)
        outs.append(jnp.concatenate([top, low], axis=0))
    return outs


def inverse_kernel(place, *refs):
    count = (len(refs) - 5) // 2
    sources, (a2, a2t, a1, a1t), targets, sems = (
        refs[:count],
        refs[count : count + 4],
        refs[count + 4 : -1],
        refs[-1],
    )
    copies = [
        pltpu.make_async_copy(source, target, sems.at[k])
        for k, (source, target) in enumerate(zip(sources, targets))
    ]
    for copy in copies:
        copy.start()
    copies[0].wait()
    copies[1].wait()
    x2, x1 = inverses_of([targets[0][...], targets[1][...]])
    a2[...] = x2
    a1[...] = x1
    a2t[...] = x2.T
    a1t[...] = x1.T
    for copy in copies[2:]:
        copy.wait()


def weight_kernel(place, a2, a2t, a1, a1t, d2, d1, c, l2, l1, bl, d2t, d1t, vt, w_hi, w_lo, bl_hi, bl_lo):
    n = d2.shape[0]
    d2t[...] = d2[...].T
    d1t[...] = d1[...].T
    x1 = split(a1[...])
    x2 = split(a2[...])
    cs = split(c[...])
    vt[0, :, :n] = a2t[...]
    vt[0, :, n:] = jnp.zeros((n, n), F32)
    vt[1, :, :n] = -dot3(x2, split(dot3(cs, x1))).T
    vt[1, :, n:] = a1t[...]
    w1 = dot3(x1, split(l1[...]))
    hi, lo = split(w1)
    w_hi[n:] = hi
    w_lo[n:] = lo
    hi, lo = split(dot3(x2, split(l2[...] - dot3(cs, (hi, lo)))))
    w_hi[:n] = hi
    w_lo[:n] = lo
    bl_hi[...], bl_lo[...] = split(bl[...])


def first_kernel(place, g2, g1, p2, p1, along_x, along_y):
    w = g2.shape[0]
    along_x[:w] = g1[...]
    along_x[w : 2 * w] = p2[...]
    along_x[2 * w :] = p1[...]
    along_y[...] = g2[...]


def far_kernel(place, x0, y0, x1, x3, x2, y1, y3, y2, far_x, far_y):
    w = y0.shape[0]
    for k, (fx, fy) in enumerate(((x0, y0), (x1, y1), (x2, y2), (x3, y3))):
        far_x[k * w : (k + 1) * w] = fy[...]
        far_y[k * w : (k + 1) * w] = fx[:w]


def gram_kernel(
    place, x0, y0, x1, x3, x2, y1, y3, y2, dx1, dx3, dx2, dy1, dy3, dy2, hi, lo, keep, send, p,
):
    x, y, core = (place[0], place[1], place[2])
    n = hi.shape[0] // 2
    w = y0.shape[0]

    def put(values, half, xx, yy):
        at = pl.multiple_of(half * n + ((yy & 3) * 4 + (xx & 3)) * w, w)
        h, l = split(values)
        hi[pl.ds(at, w)] = h
        lo[pl.ds(at, w)] = l

    for k, (fx, fy) in enumerate(((x0, y0), (x1, y1), (x2, y2), (x3, y3))):
        put(fy[...], 0, x, y + 4 - k)
        put(fx[:w], 1, x + 4 - k, y)
        rows = pl.ds(pl.multiple_of(((x + 4 - k) & 3) * w, w), w)
        p[0, rows] = fx[w : 2 * w]
        p[1, rows] = fx[2 * w :]
    for k, (fx, fy) in enumerate(((dx1, dy1), (dx2, dy2), (dx3, dy3))):
        for j in range(4):
            rows = slice(j * w, (j + 1) * w)
            put(fx[rows], 0, x + 3 - k, y + 4 - j)
            put(fy[rows], 1, x + 4 - j, y + 3 - k)
    both = split(jnp.concatenate([p[0], p[1]], axis=0))
    wide = dot3((hi[:n], lo[:n]), both, NT)
    tall = dot3((hi[n:], lo[n:]), split(p[1]), NT)
    half = n // 2
    packed = jnp.concatenate([wide, jnp.concatenate([tall[:half], tall[half:]], axis=1)], axis=0)
    part = packed.shape[0] // 2

    @pl.when(core == 0)
    def _():
        keep[...] = packed[:part]
        send[...] = packed[part:]

    @pl.when(core == 1)
    def _():
        keep[...] = packed[part:]
        send[...] = packed[:part]


def add_kernel(place, a, b, out):
    out[...] = a[...] + b[...]


def stack_kernel(place, a, b, c, d, out):
    out[0] = a[...]
    out[1] = b[...]
    out[2] = c[...]
    out[3] = d[...]


def below_sum_kernel(place, hi, lo, bl_hi, bl_lo, a2t, a1t, c, keep, send):
    core = place[2]
    n = a2t.shape[0]
    share = n // 4
    below = (bl_hi[...], bl_lo[...])
    q2 = dot3((hi[:n], lo[:n]), below)
    u2 = dot3f(a2t[...], q2)
    q1 = dot3((hi[n:], lo[n:]), below)
    u1 = dot3f(a1t[...], q1 - dot3f(c[...].T, u2))
    for k in range(2):

        @pl.when(core == k)
        def _():
            for r in range(4):
                ref = keep if r % 2 == k else send
                ref[r // 2, :share] = u2[r * share : (r + 1) * share]
                ref[r // 2, share:] = u1[r * share : (r + 1) * share]


def pair_kernel(place, keep, got, mine, send):
    z = place[3]
    mine[...] = (keep[pl.ds(z, 1)] + got[pl.ds(z, 1)])[0]
    send[...] = (keep[pl.ds(1 - z, 1)] + got[pl.ds(1 - z, 1)])[0]


def below_kernel(place, hi, lo, w_hi, w_lo, vt, grad, out, s2t, s1t, held, sems):
    w = s2t.shape[0]
    weights = (w_hi[...], w_lo[...])
    steps = sems.shape[0]
    tall = held.shape[0] // steps
    copies = []
    for k in range(steps):
        rows = pl.ds(k * tall, tall)
        held[rows] = grad[rows] - dot3((hi[:, rows], lo[:, rows]), weights, TN)
        copies.append(pltpu.make_async_copy(held.at[rows], out.at[rows], sems.at[k]))
        copies[-1].start()
    at = pl.multiple_of((place[1] * 4 + place[0]) * w, w)
    v = jnp.concatenate([vt[0, pl.ds(at, w)], vt[1, pl.ds(at, w)]], axis=0)
    solved = dot3(split(v), (hi[...], lo[...]))
    s2t[...] = solved[:w]
    s1t[...] = solved[w:]
    for copy in copies:
        copy.wait()


def chain_kernel(
    place, mine, other, a2, a2t, a1, a1t, d2t, d1t, c, gd2, gd1, gc, l2, l1, gl2, gl1, part, got,
    left2, left1, o_diag2, o_diag1, o_cross, whole, tall, rows2, rows1, rowsx, rowsxt,
):
    n = a2.shape[0]
    first = place[2] == 0
    quarter = n // 4
    half = n // 2
    for k, by in enumerate((0, 1, 3, 2)):
        y = (place[1] + 4 - by) & 3
        a, b = (mine[k], other[k])
        block = jnp.concatenate([jnp.where(first, a, b), jnp.where(first, b, a)], axis=0)
        whole[y] = block[:n]
        tall[y, :half] = block[n:, :quarter]
        tall[y, half:] = block[n:, quarter:]
    row, col = positions(n)
    lower = row >= col
    both = [dot3f(a2t[...], whole[y]) for y in range(4)]
    gram2 = jnp.concatenate([b[:, :quarter] for b in both], axis=1)
    gram_cross = jnp.concatenate([b[:, quarter:] for b in both], axis=1)
    tall = jnp.concatenate([tall[y] for y in range(4)], axis=1)
    below = dot3f(a1t[...], tall - dot3f(c[...].T, gram_cross))
    inner = halved(dot3f(d2t[...], gd2[...] - jnp.where(lower, gram2, 0.0)))
    spread = dot3f(dot3f(a2t[...], inner), a2[...])
    sym2 = spread + spread.T
    rows2[...] = sym2
    o_diag2[...] = halved(sym2)
    cross = dot3f(gc[...] - gram_cross - dot3f(sym2, c[...]), a1[...])
    o_cross[...] = cross
    rowsx[...] = cross
    cross_turned = cross.T
    rowsxt[...] = cross_turned
    gram1 = dot3f(cross_turned, c[...]) + below
    inner = halved(dot3f(d1t[...], gd1[...] - jnp.where(lower, gram1, 0.0)))
    spread = dot3f(dot3f(a1t[...], inner), a1[...])
    sym1 = spread + spread.T
    rows1[...] = sym1
    o_diag1[...] = halved(sym1)
    share = gl2.shape[0]
    at = pl.ds(pl.multiple_of((place[3] * 2 + place[2]) * share, share), share)
    l2s, l1s = (split(l2[...]), split(l1[...]))
    left2[...] = (
        gl2[...]
        - (part[:share] + got[:share])
        - dot3(split(rows2[at]), l2s)
        - dot3(split(rowsx[at]), l1s)
    )
    left1[...] = (
        gl1[...]
        - dot3(split(rowsxt[at]), l2s)
        - (part[share:] + got[share:])
        - dot3(split(rows1[at]), l1s)
    )


def shifted(value, axis, by):
    count = lax.axis_size(axis)
    return lax.ppermute(value, axis, [(i, (i + by) % count) for i in range(count)])


def shifts(value, axis):
    return [shifted(value, axis, k) for k in (1, 3, 2)]


def after(values, first):
    return lax.optimization_barrier((tuple(values), first))[0]


def body(d2, d1, c, l2, l1, bl, p2, p1, gd2, gd1, gc, gl2, gl1, gb, g2, g1):
    n = d2.shape[0]
    width = l2.shape[1]
    rows, w = p2.shape
    core = lax.axis_index("core")
    place = jnp.stack(
        [lax.axis_index("x"), lax.axis_index("y"), core, lax.axis_index("zlo")]
    ).astype(jnp.int32)
    along_x, along_y = call(
        first_kernel,
        "first",
        (near(3 * w, rows), near(w, rows)),
        (place, g2.T, g1.T, p2.T, p1.T),
        (),
        1.0,
        4,
    )
    xs = shifts(along_x, "x")
    ys = shifts(along_y, "y")
    square = near(n, n)
    given = after((d2, d1, c, l2, l1, bl, gd2, gd1, gc, gl2, gl1, gb), along_x)
    a2, a2t, a1, a1t, d2, d1, c, l2, l1, bl, gd2, gd1, gc, gl2, gl1, gb = call(
        inverse_kernel,
        "inverses",
        (square,) * 4 + tuple(near(*v.shape) for v in given),
        (place, *given),
        (pltpu.SemaphoreType.DMA((len(given),)),),
        4.0,
        len(given),
        pltpu.HBM,
    )
    pieces = (along_x, along_y, *xs, *ys)
    (x0,) = after((along_x,), a2)
    far_x, far_y = call(
        far_kernel, "far", (near(4 * w, rows),) * 2, (place, x0, *pieces[1:]), (), 0.6
    )
    dxs = [shifted(far_x, "x", k) for k in (1, 3)]
    dys = [shifted(far_y, "y", k) for k in (1, 3)]
    halves = (near(rows, width, dtype=BF16),) * 2
    thick = (near(2 * n, width, dtype=BF16),) * 2
    d2t, d1t, vt, w_hi, w_lo, bl_hi, bl_lo = call(
        weight_kernel,
        "weights",
        (square, square, near(2, n, 2 * n), *thick, *halves),
        (place, a2, a2t, a1, a1t, d2, d1, c, l2, l1, bl),
        (),
        2.7,
    )
    dxs.append(shifted(dxs[0], "x", 1))
    dys.append(shifted(dys[1], "y", 3))
    half = near(6 * n // 8, n // 2)
    (x0,) = after((along_x,), w_hi)
    hi, lo, keep, send = call(
        gram_kernel,
        "grams",
        (near(2 * n, rows, dtype=BF16),) * 2 + (half, half),
        (place, x0, *pieces[1:], *dxs, *dys),
        (pltpu.VMEM((2, 4 * w, rows), F32),),
        2.0,
    )
    (gram,) = call(
        add_kernel, "pair_gram", (half,), (place, keep, shifted(send, "core", 1)), (), 0.5
    )
    (below_hi,) = after((bl_hi,), gram)
    keep, send = call(
        below_sum_kernel,
        "below_sums",
        (near(2, n // 2, width),) * 2,
        (place, hi, lo, below_hi, bl_lo, a2t, a1t, c),
        (),
        3.0,
    )
    (gram,) = call(
        add_kernel,
        "row_gram",
        (half,),
        (place, *after((gram,), keep), shifted(gram, "zlo", 1)),
        (),
        0.6,
    )
    (send,) = after((send,), gram)
    part, send = call(
        pair_kernel,
        "pair_sums",
        (near(n // 2, width),) * 2,
        (place, keep, shifted(send, "core", 1)),
        (),
        0.6,
    )
    got = shifted(send, "zlo", 1)
    (gb,) = after((gb,), (send, gram))
    out_below, s2t, s1t = call(
        below_kernel,
        "below_outputs",
        (shaped(rows, width), shaped(w, rows), shaped(w, rows)),
        (place, hi, lo, w_hi, w_lo, vt, gb),
        (pltpu.VMEM(gb.shape, F32), pltpu.SemaphoreType.DMA((4,))),
        3.8,
        out_specs=[pl.BlockSpec(memory_space=pltpu.HBM), VMEM, VMEM],
    )
    (mine,) = call(
        stack_kernel,
        "stack",
        (near(4, *half.shape),),
        (place, *after((gram,), (s2t, got)), *shifts(gram, "y")),
        (),
        0.8,
    )
    left2, left1, diag2, diag1, cross = call(
        chain_kernel,
        "chain",
        (shaped(*gl2.shape), shaped(*gl2.shape), shaped(n, n), shaped(n, n), shaped(n, n)),
        (place, mine, shifted(mine, "core", 1), a2, a2t, a1, a1t, d2t, d1t, c, gd2, gd1, gc, l2, l1, gl2, gl1, part, got),
        (pltpu.VMEM((4, n, n // 2), F32), pltpu.VMEM((4, n, n // 4), F32))
        + (pltpu.VMEM((n, n), F32),) * 4,
        5.2,
    )
    return out_below, left2, left1, diag2, diag1, cross, s2t.T, s1t.T


def solution(mesh):
    fine = Mesh(
        mesh.devices.reshape(2, 2, 4, 4, 4), ("zlo", "core", "y", "x", "dep")
    )
    row, col, deep = (("zlo", "core"), ("y", "x"), ("y", "x", "dep"))
    return jax.shard_map(
        body,
        mesh=fine,
        in_specs=(
            P(),
            P(),
            P(),
            P(None, deep),
            P(None, deep),
            P(row, deep),
            P(row, col),
            P(row, col),
            P(),
            P(),
            P(),
            P(row, deep),
            P(row, deep),
            P(row, deep),
            P(row, col),
            P(row, col),
        ),
        out_specs=(
            P(row, deep),
            P(row, deep),
            P(row, deep),
            P(),
            P(),
            P(),
            P(row, col),
            P(row, col),
        ),
        check_vma=False,
    )
```
